128 devices in a mesh: seq: 32 (over x, y, core), head: 4 (over z).
Axes of the slice: x: 4, y: 4, z: 4, core: 2. Of those that a mesh axis runs over, the one named last changes fastest.
Arguments:
- inputs: bfloat16 [65536, 2048], P('seq'), may hold values from -6 to 6
- w_qkv: bfloat16 [3, 2048, 2048], P(None, None, 'head'), may hold values from -0.125 to 0.125
- norm_gain: float32 [2048], P('head'), may hold values from 0.1 to 1.9
- w_out: bfloat16 [2048, 2048], P('head'), may hold values from -0.125 to 0.125
Outputs:
- mixed: bfloat16 [65536, 2048], P(('seq', 'head'))
The draws below stay inside these ranges and needn't reach their ends.
All inputs are finite; a program needn't handle non-finite values.
Results may differ from the reference program's by a relative error of at most 0.0067.
Values may be sent and summed in bfloat16 or wider, within the bound.
No kernel may reach another device: no remote copies, remote signals or barrier semaphores. Data moves between devices by JAX's collectives and lax.ppermute only.
A program may use at most 128 MiB of HBM per device.

```python
import jax
import jax.numpy as jnp
from jax import lax

D = 2048
H = 16
DH = 128
BLK = 256
TOKENS = 65536
HD = 2048


def steps_of(stream_key, shape, shards, least, top_value):
    def one(dim, shards_of):
        steps = jax.random.uniform(jax.random.fold_in(jax.random.fold_in(stream_key, 6), dim), (shards_of,), jnp.float32, least / len(shards), top_value / len(shards))
        return jnp.repeat(jnp.exp(steps), shape[dim] // shards_of).reshape((-1,) + (1,) * (len(shape) - dim - 1))

    level = one(*shards[0])
    for cut in shards[1:]:
        level = level * one(*cut)
    return level


def noise(own_key, shape, width, limit, cuts=(), kind=jnp.bfloat16):
    array = width * jax.random.normal(own_key, shape, jnp.float32)
    if cuts:
        array = array * steps_of(own_key, shape, cuts, -0.22, 0.18)
    return jnp.clip(array, -limit, limit).astype(kind)


def setup_inputs(seed: int = 0) -> dict:
    seeds = jax.random.split(jax.random.key(seed), 5)
    inputs = noise(seeds[0], (TOKENS, D), 1.0, 6.0, ((0, 32),))
    w_qkv = noise(seeds[1], (3, D, HD), D ** -0.5, 0.125, ((2, 4),))
    norm_gain = jnp.clip(1.0 + 0.18 * jax.random.normal(seeds[2], (HD,), jnp.float32), 0.1, 1.9)
    w_out = noise(seeds[3], (HD, D), HD ** -0.5, 0.125, ((0, 4),))
    return dict(inputs=inputs, w_qkv=w_qkv, norm_gain=norm_gain, w_out=w_out)


def reference(inputs, w_qkv, norm_gain, w_out):
    hp = lax.Precision.HIGHEST
    q = jnp.dot(inputs, w_qkv[0], preferred_element_type=jnp.float32).astype(jnp.bfloat16)
    k = jnp.dot(inputs, w_qkv[1], preferred_element_type=jnp.float32).astype(jnp.bfloat16)
    v = jnp.dot(inputs, w_qkv[2], preferred_element_type=jnp.float32).astype(jnp.bfloat16)
    count = q.shape[0] // BLK

    def split(arr):
        return arr.reshape(count, BLK, H, DH).transpose(0, 2, 1, 3)
    lower = jnp.tril(jnp.ones((BLK, BLK), jnp.bool_))

    def advance(state, block):
        qb, kb, vb = block
        qf = qb.astype(jnp.float32)
        kf = kb.astype(jnp.float32)
        vf = vb.astype(jnp.float32)
        scores = jnp.einsum('hid,hjd->hij', qf, kf, precision=hp)
        scores = jnp.where(lower[None], scores, 0.0).astype(jnp.bfloat16)
        intra = jnp.einsum('hij,hjd->hid', scores.astype(jnp.float32), vf, precision=hp)
        inter = jnp.einsum('hid,hde->hie', qf, state, precision=hp)
        state = state + jnp.einsum('hjd,hje->hde', kf, vf, precision=hp)
        return (state, intra + inter)
    start = jnp.zeros((H, DH, DH), jnp.float32)
    final, attended = lax.scan(advance, start, (split(q), split(k), split(v)))
    mean_sq = lax.optimization_barrier(jnp.mean(attended * attended, axis=-1, keepdims=True))
    gain = norm_gain.reshape(H, 1, DH)
    normed = (attended / jnp.sqrt(mean_sq + 1e-06) * gain).astype(jnp.bfloat16)
    normed = normed.transpose(0, 2, 1, 3).reshape(count * BLK, H * DH)
    return jnp.dot(normed, w_out, preferred_element_type=jnp.float32).astype(jnp.bfloat16)
```

```python
import functools

import jax
import jax.numpy as jnp
from jax import lax
from jax.experimental import pallas as pl
from jax.experimental.pallas import tpu as pltpu
from jax.sharding import PartitionSpec as P

DH = 128
BLK = 256
F32 = jnp.float32
BF16 = jnp.bfloat16


def dot(a, b):
    return jnp.dot(a, b, preferred_element_type=F32)


def cost(flops, nbytes):
    return pl.CostEstimate(flops=int(flops), bytes_accessed=int(nbytes), transcendentals=0)


def hi_lo(state):
    high = state.astype(BF16)
    low = (state - high.astype(F32)).astype(BF16)
    return jnp.concatenate([high, low], axis=0)


def kv_kernel(x_ref, wk_ref, wv_ref, k_ref, v_ref, pre_ref, tot_ref, acc):
    step = pl.program_id(0)

    @pl.when(step == 0)
    def _():
        acc[...] = jnp.zeros_like(acc)

    x = x_ref[...]
    k_ref[...] = dot(x, wk_ref[0]).astype(BF16)
    v_ref[...] = dot(x, wv_ref[0]).astype(BF16)
    heads = acc.shape[0]
    for b in range(x.shape[0] // BLK):
        rows = slice(b * BLK, (b + 1) * BLK)
        for h in range(heads):
            cols = slice(h * DH, (h + 1) * DH)
            before = acc[h]
            pre_ref[b, h] = hi_lo(before)
            acc[h] = before + lax.dot_general(
                k_ref[rows, cols], v_ref[rows, cols], (((0,), (0,)), ((), ())),
                preferred_element_type=F32,
            )

    @pl.when(step == pl.num_programs(0) - 1)
    def _():
        tot_ref[...] = acc[...]


def project_kv(x, w_qkv, tile=512):
    tokens, width = x.shape
    feats = w_qkv.shape[2]
    heads = feats // DH
    blocks = tile // BLK
    return pl.pallas_call(
        kv_kernel,
        grid=(tokens // tile,),
        in_specs=[
            pl.BlockSpec((tile, width), lambda i: (i, 0)),
            pl.BlockSpec((1, width, feats), lambda i: (1, 0, 0)),
            pl.BlockSpec((1, width, feats), lambda i: (2, 0, 0)),
        ],
        out_specs=[
            pl.BlockSpec((tile, feats), lambda i: (i, 0)),
            pl.BlockSpec((tile, feats), lambda i: (i, 0)),
            pl.BlockSpec((blocks, heads, 2 * DH, DH), lambda i: (i, 0, 0, 0)),
            pl.BlockSpec((heads, DH, DH), lambda i: (0, 0, 0)),
        ],
        out_shape=[
            jax.ShapeDtypeStruct((tokens, feats), BF16),
            jax.ShapeDtypeStruct((tokens, feats), BF16),
            jax.ShapeDtypeStruct((tokens // BLK, heads, 2 * DH, DH), BF16),
            jax.ShapeDtypeStruct((heads, DH, DH), F32),
        ],
        scratch_shapes=[pltpu.VMEM((heads, DH, DH), F32)],
        cost_estimate=cost(4 * tokens * width * feats, 2 * tokens * width + 4 * width * feats),
        name="project_kv",
    )(x, w_qkv, w_qkv)


def local_kernel(x_ref, wq_ref, k_ref, v_ref, pre_ref, q_ref, att_ref):
    q_ref[...] = dot(x_ref[...], wq_ref[0]).astype(BF16)
    heads = pre_ref.shape[1]
    lower = lax.broadcasted_iota(jnp.int32, (BLK, BLK), 0) >= lax.broadcasted_iota(
        jnp.int32, (BLK, BLK), 1
    )
    for b in range(x_ref.shape[0] // BLK):
        rows = slice(b * BLK, (b + 1) * BLK)
        for h in range(heads):
            cols = slice(h * DH, (h + 1) * DH)
            q = q_ref[rows, cols]
            scores = lax.dot_general(
                q, k_ref[rows, cols], (((1,), (1,)), ((), ())), preferred_element_type=F32
            )
            scores = jnp.where(lower, scores, 0.0).astype(BF16)
            att_ref[rows, cols] = dot(scores, v_ref[rows, cols]) + dot(
                jnp.concatenate([q, q], axis=1), pre_ref[b, h]
            )


def local_part(x, w_qkv, k, v, pre, first, count, tile=256):
    tokens, width = x.shape
    feats = w_qkv.shape[2]
    heads = feats // DH
    blocks = tile // BLK
    start = first // tile
    row = lambda i: (i + start, 0)
    return pl.pallas_call(
        local_kernel,
        grid=(count // tile,),
        in_specs=[
            pl.BlockSpec((tile, width), row),
            pl.BlockSpec((1, width, feats), lambda i: (0, 0, 0)),
            pl.BlockSpec((tile, feats), row),
            pl.BlockSpec((tile, feats), row),
            pl.BlockSpec((blocks, heads, 2 * DH, DH), lambda i: (i + start, 0, 0, 0)),
        ],
        out_specs=[
            pl.BlockSpec((tile, feats), lambda i: (i, 0)),
            pl.BlockSpec((tile, feats), lambda i: (i, 0)),
        ],
        out_shape=[
            jax.ShapeDtypeStruct((count, feats), BF16),
            jax.ShapeDtypeStruct((count, feats), F32),
        ],
        cost_estimate=cost(2 * count * feats * (width + 4 * BLK), 2 * count * width + 2 * width * feats),
        name="local_part",
    )(x, w_qkv, k, v, pre)


def finish_kernel(place, q_ref, att_ref, carried_ref, gain_ref, n_ref):
    heads = carried_ref.shape[0]
    for h in range(heads):
        cols = slice(h * DH, (h + 1) * DH)
        q = q_ref[:, cols]
        att = att_ref[:, cols] + dot(jnp.concatenate([q, q], axis=1), hi_lo(carried_ref[h]))
        mean_sq = jnp.mean(att * att, axis=-1, keepdims=True)
        n_ref[:, cols] = (att / jnp.sqrt(mean_sq + 1e-06) * gain_ref[:, cols]).astype(BF16)


def finish(place, q, att, carried, gain, shift, parts, tile=256):
    tokens, feats = q.shape
    count = tokens // parts
    per = count // tile
    heads = feats // DH
    row = lambda i, place: (lax.rem(place[0] + shift, parts) * per + i, 0)
    return pl.pallas_call(
        finish_kernel,
        grid_spec=pltpu.PrefetchScalarGridSpec(
            num_scalar_prefetch=1,
            grid=(per,),
            in_specs=[
                pl.BlockSpec((tile, feats), row),
                pl.BlockSpec((tile, feats), row),
                pl.BlockSpec((heads, DH, DH), lambda i, place: (0, 0, 0)),
                pl.BlockSpec((1, feats), lambda i, place: (0, 0)),
            ],
            out_specs=pl.BlockSpec((tile, feats), lambda i, place: (i, 0)),
        ),
        out_shape=jax.ShapeDtypeStruct((count, feats), BF16),
        cost_estimate=cost(2 * count * feats * DH * 2, count * feats * 8),
        name="finish",
    )(place, q, att, carried, gain)


def mix_kernel(core, n0, nl, nr, nf, w0, wl, ol, wr, orr, wt, wb, ot, ob, out_ref):
    half = wl.shape[0]
    mine = pl.multiple_of(core[0] * half, half)
    other = pl.multiple_of((1 - core[0]) * half, half)
    acc = dot(n0[...], w0[...])
    acc += dot(nl[:, pl.ds(mine, half)], wl[...]) + dot(nl[:, pl.ds(other, half)], ol[...])
    acc += dot(nr[:, pl.ds(mine, half)], wr[...]) + dot(nr[:, pl.ds(other, half)], orr[...])
    far = jnp.concatenate([wt[...], wb[...]], axis=0)
    acc += dot(nf[:, pl.ds(mine, half)], far)
    far = jnp.concatenate([ot[...], ob[...]], axis=0)
    acc += dot(nf[:, pl.ds(other, half)], far)
    out_ref[...] = acc.astype(BF16)


def mix(core, normed, weights, tile=512):
    rows, feats = normed[0].shape
    width = weights[0].shape[1]
    whole = lambda a: pl.BlockSpec(a.shape, lambda i, core: (0, 0))
    part = lambda a: pl.BlockSpec((a.shape[0], tile), lambda i, core: (0, i))
    return pl.pallas_call(
        mix_kernel,
        grid_spec=pltpu.PrefetchScalarGridSpec(
            num_scalar_prefetch=1,
            grid=(width // tile,),
            in_specs=[whole(a) for a in normed] + [part(a) for a in weights],
            out_specs=pl.BlockSpec((rows, tile), lambda i, core: (0, i)),
        ),
        out_shape=jax.ShapeDtypeStruct((rows, width), BF16),
        cost_estimate=cost(8 * rows * feats * width, 10 * rows * width),
        name="mix",
    )(core, *normed, *weights)


def seq_shift(axis_stride, size, total, shift):
    pairs = []
    for i in range(total):
        at = (i // axis_stride) % size
        pairs.append((i, i + ((at + shift) % size - at) * axis_stride))
    return pairs


def earlier_and_all(value, position, size, stride, total):
    before = jnp.zeros(value.shape, F32)
    every = value.astype(F32)
    got = []
    for shift in (2, 1, 3):
        got.append((shift, lax.ppermute(value, "seq", seq_shift(stride, size, total, shift))))
    for shift, other in got:
        other = other.astype(F32)
        source = lax.rem(position - shift + size, size)
        before = before + jnp.where(source < position, other, 0.0)
        every = every + other
    return before, every


def on_device(inputs, w_qkv, norm_gain, w_out):
    parts = lax.axis_size("head")
    total = lax.axis_size("seq")
    seq = lax.axis_index("seq")
    core = lax.rem(seq, 2)
    y = lax.rem(seq // 2, 4)
    x = seq // 8
    place = lax.axis_index("head").astype(jnp.int32).reshape(1)
    core_id = core.astype(jnp.int32).reshape(1)
    up = [(i, (i + 1) % parts) for i in range(parts)]
    down = [(i, (i - 1) % parts) for i in range(parts)]
    across = [(i, (i + 2) % parts) for i in range(parts)]
    partner = [(i, i ^ 1) for i in range(total)]

    rows = w_out.shape[0] // 2
    own = lax.dynamic_slice_in_dim(w_out, core * rows, rows, 0)
    from_low = lax.ppermute(own, "head", up)
    from_high = lax.ppermute(own, "head", down)
    far_top = lax.ppermute(from_low[: rows // 2], "head", up)
    far_bottom = lax.ppermute(from_high[rows // 2 :], "head", down)

    def swap(a):
        return lax.ppermute(a, "seq", partner)

    k, v, pre, tot = project_kv(inputs, w_qkv)
    other = swap(tot)
    q, att = local_part(inputs, w_qkv, k, v, pre, 0, inputs.shape[0])
    carried = jnp.where(core == 1, other, 0.0)
    chip = (tot + other).astype(BF16)
    before, every = earlier_and_all(chip, y, 4, 2, total)
    carried = carried + before
    before, _ = earlier_and_all(every.astype(BF16), x, 4, 8, total)
    carried = carried + before

    gain = norm_gain.reshape(1, -1)
    n2 = finish(place, q, att, carried, gain, 2, parts)
    n1 = finish(place, q, att, carried, gain, 1, parts)
    n3 = finish(place, q, att, carried, gain, 3, parts)
    n0 = finish(place, q, att, carried, gain, 0, parts)
    nf = lax.ppermute(n2, "head", across)
    nl = lax.ppermute(n1, "head", up)
    nr = lax.ppermute(n3, "head", down)
    weights = [
        w_out,
        from_low, swap(from_low),
        from_high, swap(from_high),
        far_top, far_bottom, swap(far_top), swap(far_bottom),
    ]
    return mix(core_id, [n0, nl, nr, nf], weights)


def solution(mesh):
    return jax.shard_map(
        on_device,
        mesh=mesh,
        in_specs=(P("seq", None), P(None, None, "head"), P("head"), P("head", None)),
        out_specs=P(("seq", "head"), None),
        check_vma=False,
    )
```

```python
import jax
import jax.numpy as jnp
from jax import lax
from jax.experimental import pallas as pl
from jax.experimental.pallas import tpu as pltpu
from jax.sharding import PartitionSpec as P


DH = 128
BLK = 256
F32 = jnp.float32
BF16 = jnp.bfloat16


def dot(a, b):
    return jnp.dot(a, b, preferred_element_type=F32)


def cost(flops, nbytes):
    return pl.CostEstimate(flops=int(flops), bytes_accessed=int(nbytes), transcendentals=0)


def hi_lo(state):
    high = state.astype(BF16)
    low = (state - high.astype(F32)).astype(BF16)
    return jnp.concatenate([high, low], axis=0)


def qkv_kernel(x_ref, wq_ref, wk_ref, wv_ref, q_ref, k_ref, v_ref, pre_ref, tot_ref, acc):
    step = pl.program_id(0)

    @pl.when(step == 0)
    def _():
        acc[...] = jnp.zeros_like(acc)

    x = x_ref[...]
    k_ref[...] = dot(x, wk_ref[0]).astype(BF16)
    v_ref[...] = dot(x, wv_ref[0]).astype(BF16)
    q_ref[...] = dot(x, wq_ref[0]).astype(BF16)
    heads = acc.shape[0]
    for b in range(x.shape[0] // BLK):
        rows = slice(b * BLK, (b + 1) * BLK)
        for h in range(heads):
            cols = slice(h * DH, (h + 1) * DH)
            before = acc[h]
            pre_ref[b, h] = hi_lo(before)
            acc[h] = before + lax.dot_general(
                k_ref[rows, cols], v_ref[rows, cols], (((0,), (0,)), ((), ())),
                preferred_element_type=F32,
            )

    @pl.when(step == pl.num_programs(0) - 1)
    def _():
        tot_ref[...] = acc[...]


def project(x, w_qkv, tile=512):
    tokens, width = x.shape
    feats = w_qkv.shape[2]
    heads = feats // DH
    blocks = tile // BLK
    weight = lambda which: pl.BlockSpec((1, width, feats), lambda i: (which, 0, 0))
    rows = pl.BlockSpec((tile, feats), lambda i: (i, 0))
    return pl.pallas_call(
        qkv_kernel,
        grid=(tokens // tile,),
        in_specs=[pl.BlockSpec((tile, width), lambda i: (i, 0)), weight(0), weight(1), weight(2)],
        out_specs=[
            rows,
            rows,
            rows,
            pl.BlockSpec((blocks, heads, 2 * DH, DH), lambda i: (i, 0, 0, 0)),
            pl.BlockSpec((heads, DH, DH), lambda i: (0, 0, 0)),
        ],
        out_shape=[jax.ShapeDtypeStruct((tokens, feats), BF16)] * 3
        + [
            jax.ShapeDtypeStruct((tokens // BLK, heads, 2 * DH, DH), BF16),
            jax.ShapeDtypeStruct((heads, DH, DH), F32),
        ],
        scratch_shapes=[pltpu.VMEM((heads, DH, DH), F32)],
        cost_estimate=cost(6 * tokens * width * feats, 2 * tokens * width + 6 * width * feats),
        name="project",
    )(x, w_qkv, w_qkv, w_qkv)


def local_kernel(q_ref, k_ref, v_ref, pre_ref, *rest):
    att_ref = rest[-1]
    heads = pre_ref.shape[1]
    lower = lax.broadcasted_iota(jnp.int32, (BLK, BLK), 0) >= lax.broadcasted_iota(
        jnp.int32, (BLK, BLK), 1
    )
    for b in range(q_ref.shape[0] // BLK):
        rows = slice(b * BLK, (b + 1) * BLK)
        for h in range(heads):
            cols = slice(h * DH, (h + 1) * DH)
            q = q_ref[rows, cols]
            scores = lax.dot_general(
                q, k_ref[rows, cols], (((1,), (1,)), ((), ())), preferred_element_type=F32
            )
            scores = jnp.where(lower, scores, 0.0).astype(BF16)
            att_ref[rows, cols] = dot(scores, v_ref[rows, cols]) + dot(
                jnp.concatenate([q, q], axis=1), pre_ref[b, h]
            )


def local_part(q, k, v, pre, att, piece, pieces, tile=256):
    tokens, feats = q.shape
    heads = feats // DH
    blocks = tile // BLK
    count = tokens // pieces
    start = piece * count // tile
    row = pl.BlockSpec((tile, feats), lambda i: (i + start, 0))
    return pl.pallas_call(
        local_kernel,
        grid=(count // tile,),
        in_specs=[
            row, row, row,
            pl.BlockSpec((blocks, heads, 2 * DH, DH), lambda i: (i + start, 0, 0, 0)),
        ]
        + [pl.BlockSpec(memory_space=pl.ANY)] * len(att),
        out_specs=row,
        out_shape=jax.ShapeDtypeStruct((tokens, feats), F32),
        input_output_aliases={4: 0} if att else {},
        cost_estimate=cost(8 * count * feats * BLK, 14 * count * feats),
        name="local_part",
    )(q, k, v, pre, *att)


def finish_kernel(place, q_ref, att_ref, carried_ref, gain_ref, n_ref):
    heads = carried_ref.shape[0]
    for h in range(heads):
        cols = slice(h * DH, (h + 1) * DH)
        q = q_ref[:, cols]
        att = att_ref[:, cols] + dot(jnp.concatenate([q, q], axis=1), hi_lo(carried_ref[h]))
        mean_sq = jnp.mean(att * att, axis=-1, keepdims=True)
        n_ref[:, cols] = (att / jnp.sqrt(mean_sq + 1e-06) * gain_ref[:, cols]).astype(BF16)


def finish(place, q, att, carried, gain, parts, tile=256):
    tokens, feats = q.shape
    count = tokens // parts
    per = count // tile
    heads = feats // DH
    row = lambda i, place: (place[0] * per + i, 0)
    return pl.pallas_call(
        finish_kernel,
        grid_spec=pltpu.PrefetchScalarGridSpec(
            num_scalar_prefetch=1,
            grid=(per,),
            in_specs=[
                pl.BlockSpec((tile, feats), row),
                pl.BlockSpec((tile, feats), row),
                pl.BlockSpec((heads, DH, DH), lambda i, place: (0, 0, 0)),
                pl.BlockSpec((1, feats), lambda i, place: (0, 0)),
            ],
            out_specs=pl.BlockSpec((tile, feats), lambda i, place: (i, 0)),
        ),
        out_shape=jax.ShapeDtypeStruct((count, feats), BF16),
        cost_estimate=cost(2 * count * feats * DH * 2, count * feats * 8),
        name="finish",
    )(place, q, att, carried, gain)


def near_kernel(n0, na, nb, w0, wa, wb, acc_ref):
    acc_ref[...] = dot(n0[...], w0[...]) + dot(na[...], wa[...]) + dot(nb[...], wb[...])


def far_kernel(core, acc_ref, nf, mine_ref, other_ref, out_ref):
    half = mine_ref.shape[0]
    mine = pl.multiple_of(core[0] * half, half)
    other = pl.multiple_of((1 - core[0]) * half, half)
    acc = acc_ref[...] + dot(nf[:, pl.ds(mine, half)], mine_ref[...])
    acc += dot(nf[:, pl.ds(other, half)], other_ref[...])
    out_ref[...] = acc.astype(BF16)


def mix_near(normed, weights, tile=512):
    rows, feats = normed[0].shape
    width = weights[0].shape[1]
    return pl.pallas_call(
        near_kernel,
        grid=(width // tile,),
        in_specs=[pl.BlockSpec(a.shape, lambda i: (0, 0)) for a in normed]
        + [pl.BlockSpec((a.shape[0], tile), lambda i: (0, i)) for a in weights],
        out_specs=pl.BlockSpec((rows, tile), lambda i: (0, i)),
        out_shape=jax.ShapeDtypeStruct((rows, width), F32),
        cost_estimate=cost(6 * rows * feats * width, 10 * rows * width),
        compiler_params=pltpu.CompilerParams(vmem_limit_bytes=24 << 20),
        name="mix_near",
    )(*normed, *weights)


def mix_far(core, acc, normed, weights, tile=512):
    rows, feats = normed.shape
    width = acc.shape[1]
    column = lambda a: pl.BlockSpec((a.shape[0], tile), lambda i, core: (0, i))
    return pl.pallas_call(
        far_kernel,
        grid_spec=pltpu.PrefetchScalarGridSpec(
            num_scalar_prefetch=1,
            grid=(width // tile,),
            in_specs=[column(acc), pl.BlockSpec(normed.shape, lambda i, core: (0, 0))]
            + [column(a) for a in weights],
            out_specs=pl.BlockSpec((rows, tile), lambda i, core: (0, i)),
        ),
        out_shape=jax.ShapeDtypeStruct((rows, width), BF16),
        cost_estimate=cost(2 * rows * feats * width, 8 * rows * width),
        compiler_params=pltpu.CompilerParams(vmem_limit_bytes=24 << 20),
        name="mix_far",
    )(core, acc, normed, *weights)


def pair_up(size, stride, total, first):
    pairs = []
    for i in range(total):
        at = (i // stride) % size
        to = at ^ 1 if first else (at + (1 if at % 2 else -1)) % size
        pairs.append((i, i + (to - at) * stride))
    return pairs


def exclusive_prefix(value, position, stride, total):
    other = lax.ppermute(value.astype(BF16), "seq", pair_up(4, stride, total, True))
    other = other.astype(F32)
    value = value.astype(BF16).astype(F32)
    pair = value + other
    odd = lax.rem(position, 2) == 1
    before = jnp.where(odd, other, 0.0)
    far = lax.ppermute(pair.astype(BF16), "seq", pair_up(4, stride, total, False))
    far = far.astype(F32)
    return before + jnp.where(position >= 2, far, 0.0), pair + far


def layer(inputs, w_qkv, norm_gain, w_out):
    parts = lax.axis_size("head")
    total = lax.axis_size("seq")
    seq = lax.axis_index("seq")
    core = lax.rem(seq, 2)
    y = lax.rem(seq // 2, 4)
    x = seq // 8
    head = lax.axis_index("head")
    core_id = core.astype(jnp.int32).reshape(1)
    step = 1 - 2 * core

    def place(shift):
        return lax.rem(head + shift + parts, parts).astype(jnp.int32).reshape(1)

    def along(direction):
        pairs = []
        for i in range(total):
            shift = direction * (1 - 2 * (i % 2))
            for h in range(parts):
                pairs.append((i * parts + h, i * parts + (h + shift) % parts))
        return pairs

    partner = [(i, i ^ 1) for i in range(total)]
    across = [(i, (i + 2) % parts) for i in range(parts)]

    def swap(a):
        return lax.ppermute(a, "seq", partner)

    def send(a, direction):
        return lax.ppermute(a, ("seq", "head"), along(direction))

    near = send(w_out, 1)
    rows = w_out.shape[0] // 2
    far = send(lax.dynamic_slice_in_dim(near, core * rows, rows, 0), 1)
    near_other = swap(near)
    far_other = swap(far)

    q, k, v, pre, tot = project(inputs, w_qkv)
    other = swap(tot)
    att = []
    for piece in range(4):
        att = [local_part(q, k, v, pre, att, piece, 4)]
    att = att[0]
    before, row = exclusive_prefix(tot + other, y, 2, total)
    carried = jnp.where(core == 1, other, 0.0) + before
    before, _ = exclusive_prefix(row, x, 8, total)
    carried = carried + before

    gain = norm_gain.reshape(1, -1)
    na = send(finish(place(step), q, att, carried, gain, parts), 1)
    nb = send(finish(place(-step), q, att, carried, gain, parts), -1)
    nf = finish(place(2), q, att, carried, gain, parts)
    nf = lax.ppermute(nf, "head", across)
    n0 = finish(place(0), q, att, carried, gain, parts)
    acc = mix_near([n0, na, nb], [w_out, near, near_other])
    return mix_far(core_id, acc, nf, [far, far_other])


def solution(mesh):
    return jax.shard_map(
        layer,
        mesh=mesh,
        in_specs=(P("seq", None), P(None, None, "head"), P("head"), P("head", None)),
        out_specs=P(("seq", "head"), None),
        check_vma=False,
    )
```

```python
import jax
import jax.numpy as jnp
from jax import lax
from jax.experimental import pallas as pl
from jax.experimental.pallas import tpu as pltpu
from jax.sharding import PartitionSpec as P


DH = 128
BLK = 256
F32 = jnp.float32
BF16 = jnp.bfloat16


def dot(a, b):
    return jnp.dot(a, b, preferred_element_type=F32)


def cost(flops, nbytes):
    return pl.CostEstimate(flops=int(flops), bytes_accessed=int(nbytes), transcendentals=0)


def hi_lo(state):
    high = state.astype(BF16)
    low = (state - high.astype(F32)).astype(BF16)
    return jnp.concatenate([high, low], axis=0)


def qkv_kernel(x_ref, wq_ref, wk_ref, wv_ref, q_ref, k_ref, v_ref, pre_ref, tot_ref, acc):
    step = pl.program_id(0)

    @pl.when(step == 0)
    def _():
        acc[...] = jnp.zeros_like(acc)

    x = x_ref[...]
    k_ref[...] = dot(x, wk_ref[0]).astype(BF16)
    v_ref[...] = dot(x, wv_ref[0]).astype(BF16)
    q_ref[...] = dot(x, wq_ref[0]).astype(BF16)
    heads = acc.shape[0]
    for b in range(x.shape[0] // BLK):
        rows = slice(b * BLK, (b + 1) * BLK)
        for h in range(heads):
            cols = slice(h * DH, (h + 1) * DH)
            before = acc[h]
            pre_ref[b, h] = hi_lo(before)
            acc[h] = before + lax.dot_general(
                k_ref[rows, cols], v_ref[rows, cols], (((0,), (0,)), ((), ())),
                preferred_element_type=F32,
            )

    @pl.when(step == pl.num_programs(0) - 1)
    def _():
        tot_ref[...] = acc[...]


def project(x, w_qkv, tile=512):
    tokens, width = x.shape
    feats = w_qkv.shape[2]
    heads = feats // DH
    blocks = tile // BLK
    weight = lambda which: pl.BlockSpec((1, width, feats), lambda i: (which, 0, 0))
    rows = pl.BlockSpec((tile, feats), lambda i: (i, 0))
    return pl.pallas_call(
        qkv_kernel,
        grid=(tokens // tile,),
        in_specs=[pl.BlockSpec((tile, width), lambda i: (i, 0)), weight(0), weight(1), weight(2)],
        out_specs=[
            rows,
            rows,
            rows,
            pl.BlockSpec((blocks, heads, 2 * DH, DH), lambda i: (i, 0, 0, 0)),
            pl.BlockSpec((heads, DH, DH), lambda i: (0, 0, 0)),
        ],
        out_shape=[jax.ShapeDtypeStruct((tokens, feats), BF16)] * 3
        + [
            jax.ShapeDtypeStruct((tokens // BLK, heads, 2 * DH, DH), BF16),
            jax.ShapeDtypeStruct((heads, DH, DH), F32),
        ],
        scratch_shapes=[pltpu.VMEM((heads, DH, DH), F32)],
        cost_estimate=cost(6 * tokens * width * feats, 2 * tokens * width + 6 * width * feats),
        name="project",
    )(x, w_qkv, w_qkv, w_qkv)


def local_kernel(q_ref, k_ref, v_ref, pre_ref, *rest):
    att_ref = rest[-1]
    heads = pre_ref.shape[1]
    lower = lax.broadcasted_iota(jnp.int32, (BLK, BLK), 0) >= lax.broadcasted_iota(
        jnp.int32, (BLK, BLK), 1
    )
    for b in range(q_ref.shape[0] // BLK):
        rows = slice(b * BLK, (b + 1) * BLK)
        for h in range(heads):
            cols = slice(h * DH, (h + 1) * DH)
            q = q_ref[rows, cols]
            scores = lax.dot_general(
                q, k_ref[rows, cols], (((1,), (1,)), ((), ())), preferred_element_type=F32
            )
            scores = jnp.where(lower, scores, 0.0).astype(BF16)
            att_ref[rows, cols] = dot(scores, v_ref[rows, cols]) + dot(
                jnp.concatenate([q, q], axis=1), pre_ref[b, h]
            )


def local_part(q, k, v, pre, att, piece, pieces, tile=256):
    tokens, feats = q.shape
    heads = feats // DH
    blocks = tile // BLK
    count = tokens // pieces
    start = piece * count // tile
    row = pl.BlockSpec((tile, feats), lambda i: (i + start, 0))
    return pl.pallas_call(
        local_kernel,
        grid=(count // tile,),
        in_specs=[
            row, row, row,
            pl.BlockSpec((blocks, heads, 2 * DH, DH), lambda i: (i + start, 0, 0, 0)),
        ]
        + [pl.BlockSpec(memory_space=pl.ANY)] * len(att),
        out_specs=row,
        out_shape=jax.ShapeDtypeStruct((tokens, feats), F32),
        input_output_aliases={4: 0} if att else {},
        cost_estimate=cost(8 * count * feats * BLK, 14 * count * feats),
        name="local_part",
    )(q, k, v, pre, *att)


def finish_kernel(place, q_ref, att_ref, carried_ref, gain_ref, n_ref):
    heads = carried_ref.shape[0]
    for h in range(heads):
        cols = slice(h * DH, (h + 1) * DH)
        q = q_ref[:, cols]
        att = att_ref[:, cols] + dot(jnp.concatenate([q, q], axis=1), hi_lo(carried_ref[h]))
        mean_sq = jnp.mean(att * att, axis=-1, keepdims=True)
        n_ref[:, cols] = (att / jnp.sqrt(mean_sq + 1e-06) * gain_ref[:, cols]).astype(BF16)


def finish(place, q, att, carried, gain, parts, tile=256):
    tokens, feats = q.shape
    count = tokens // parts
    per = count // tile
    heads = feats // DH
    row = lambda i, place: (place[0] * per + i, 0)
    return pl.pallas_call(
        finish_kernel,
        grid_spec=pltpu.PrefetchScalarGridSpec(
            num_scalar_prefetch=1,
            grid=(per,),
            in_specs=[
                pl.BlockSpec((tile, feats), row),
                pl.BlockSpec((tile, feats), row),
                pl.BlockSpec((heads, DH, DH), lambda i, place: (0, 0, 0)),
                pl.BlockSpec((1, feats), lambda i, place: (0, 0)),
            ],
            out_specs=pl.BlockSpec((tile, feats), lambda i, place: (i, 0)),
        ),
        out_shape=jax.ShapeDtypeStruct((count, feats), BF16),
        cost_estimate=cost(2 * count * feats * DH * 2, count * feats * 8),
        name="finish",
    )(place, q, att, carried, gain)


def near_kernel(n0, na, nb, w0, wa, wb, acc_ref):
    acc_ref[...] = dot(n0[...], w0[...]) + dot(na[...], wa[...]) + dot(nb[...], wb[...])


def far_kernel(core, acc_ref, nf, mine_ref, other_ref, out_ref):
    half = mine_ref.shape[0]
    mine = pl.multiple_of(core[0] * half, half)
    other = pl.multiple_of((1 - core[0]) * half, half)
    acc = acc_ref[...] + dot(nf[:, pl.ds(mine, half)], mine_ref[...])
    acc += dot(nf[:, pl.ds(other, half)], other_ref[...])
    out_ref[...] = acc.astype(BF16)


def mix_near(normed, weights, tile=512):
    rows, feats = normed[0].shape
    width = weights[0].shape[1]
    return pl.pallas_call(
        near_kernel,
        grid=(width // tile,),
        in_specs=[pl.BlockSpec(a.shape, lambda i: (0, 0)) for a in normed]
        + [pl.BlockSpec((a.shape[0], tile), lambda i: (0, i)) for a in weights],
        out_specs=pl.BlockSpec((rows, tile), lambda i: (0, i)),
        out_shape=jax.ShapeDtypeStruct((rows, width), F32),
        cost_estimate=cost(6 * rows * feats * width, 10 * rows * width),
        compiler_params=pltpu.CompilerParams(vmem_limit_bytes=59 << 20),
        name="mix_near",
    )(*normed, *weights)


def mix_far(core, acc, normed, weights, tile=512):
    rows, feats = normed.shape
    width = acc.shape[1]
    column = lambda a: pl.BlockSpec((a.shape[0], tile), lambda i, core: (0, i))
    return pl.pallas_call(
        far_kernel,
        grid_spec=pltpu.PrefetchScalarGridSpec(
            num_scalar_prefetch=1,
            grid=(width // tile,),
            in_specs=[column(acc), pl.BlockSpec(normed.shape, lambda i, core: (0, 0))]
            + [column(a) for a in weights],
            out_specs=pl.BlockSpec((rows, tile), lambda i, core: (0, i)),
        ),
        out_shape=jax.ShapeDtypeStruct((rows, width), BF16),
        cost_estimate=cost(2 * rows * feats * width, 8 * rows * width),
        compiler_params=pltpu.CompilerParams(vmem_limit_bytes=59 << 20),
        name="mix_far",
    )(core, acc, normed, *weights)


def pair_up(size, stride, total, first):
    pairs = []
    for i in range(total):
        at = (i // stride) % size
        to = at ^ 1 if first else (at + (1 if at % 2 else -1)) % size
        pairs.append((i, i + (to - at) * stride))
    return pairs


def exclusive_prefix(value, position, stride, total):
    other = lax.ppermute(value.astype(BF16), "seq", pair_up(4, stride, total, True))
    other = other.astype(F32)
    value = value.astype(BF16).astype(F32)
    pair = value + other
    odd = lax.rem(position, 2) == 1
    before = jnp.where(odd, other, 0.0)
    far = lax.ppermute(pair.astype(BF16), "seq", pair_up(4, stride, total, False))
    far = far.astype(F32)
    return before + jnp.where(position >= 2, far, 0.0), pair + far


def layer(inputs, w_qkv, norm_gain, w_out):
    parts = lax.axis_size("head")
    total = lax.axis_size("seq")
    seq = lax.axis_index("seq")
    core = lax.rem(seq, 2)
    y = lax.rem(seq // 2, 4)
    x = seq // 8
    head = lax.axis_index("head")
    core_id = core.astype(jnp.int32).reshape(1)
    step = 1 - 2 * core

    def place(shift):
        return lax.rem(head + shift + parts, parts).astype(jnp.int32).reshape(1)

    def along(direction):
        pairs = []
        for i in range(total):
            shift = direction * (1 - 2 * (i % 2))
            for h in range(parts):
                pairs.append((i * parts + h, i * parts + (h + shift) % parts))
        return pairs

    partner = [(i, i ^ 1) for i in range(total)]

    def swap(a):
        return lax.ppermute(a, "seq", partner)

    def send(a, direction):
        return lax.ppermute(a, ("seq", "head"), along(direction))

    near = send(w_out, 1)
    rows = w_out.shape[0] // 2
    far = send(lax.dynamic_slice_in_dim(near, core * rows, rows, 0), 1)
    near_other = swap(near)
    far_other = swap(far)

    q, k, v, pre, tot = project(inputs, w_qkv)
    other = swap(tot)
    att = []
    for piece in range(4):
        att = [local_part(q, k, v, pre, att, piece, 4)]
    att = att[0]
    before, row = exclusive_prefix(tot + other, y, 2, total)
    carried = jnp.where(core == 1, other, 0.0) + before
    before, _ = exclusive_prefix(row, x, 8, total)
    carried = carried + before

    gain = norm_gain.reshape(1, -1)
    nf = send(finish(place(2), q, att, carried, gain, parts), 1)
    na = send(finish(place(step), q, att, carried, gain, parts), 1)
    nb = send(finish(place(-step), q, att, carried, gain, parts), -1)
    nf = send(nf, 1)
    n0 = finish(place(0), q, att, carried, gain, parts)
    acc = mix_near([n0, na, nb], [w_out, near, near_other])
    return mix_far(core_id, acc, nf, [far, far_other])


def solution(mesh):
    return jax.shard_map(
        layer,
        mesh=mesh,
        in_specs=(P("seq", None), P(None, None, "head"), P("head"), P("head", None)),
        out_specs=P(("seq", "head"), None),
        check_vma=False,
    )
```

```python
import jax
import jax.numpy as jnp
from jax import lax
from jax.experimental import pallas as pl
from jax.experimental.pallas import tpu as pltpu
from jax.sharding import PartitionSpec as P


DH = 128
BLK = 256
F32 = jnp.float32
BF16 = jnp.bfloat16


def dot(a, b):
    return jnp.dot(a, b, preferred_element_type=F32)


def cost(flops, nbytes):
    return pl.CostEstimate(flops=int(flops), bytes_accessed=int(nbytes), transcendentals=0)


def hi_lo(state):
    high = state.astype(BF16)
    low = (state - high.astype(F32)).astype(BF16)
    return jnp.concatenate([high, low], axis=0)


def qkv_kernel(x_hbm, w_hbm, q_ref, k_ref, v_ref, pre_ref, tot_ref, acc, x_buf, w_buf, x_sem, w_sem):
    step = pl.program_id(0)
    steps = pl.num_programs(0)
    tile = x_buf.shape[1]

    def tokens(i):
        slot = lax.rem(i, 2)
        rows = pl.ds(pl.multiple_of(i * tile, tile), tile)
        return pltpu.make_async_copy(x_hbm.at[rows], x_buf.at[slot], x_sem.at[slot])

    def weight(which):
        return pltpu.make_async_copy(w_hbm.at[which], w_buf.at[which], w_sem.at[which])

    @pl.when(step == 0)
    def _():
        tokens(0).start()
        weight(1).start()
        weight(2).start()
        weight(0).start()
        acc[...] = jnp.zeros_like(acc)

    @pl.when(step + 1 < steps)
    def _():
        tokens(step + 1).start()

    tokens(step).wait()
    slot = lax.rem(step, 2)

    for which, out in ((1, k_ref), (2, v_ref), (0, q_ref)):

        @pl.when(step == 0)
        def _():
            weight(which).wait()

        out[...] = dot(x_buf[slot], w_buf[which]).astype(BF16)

    heads = acc.shape[0]
    for b in range(tile // BLK):
        rows = slice(b * BLK, (b + 1) * BLK)
        for h in range(heads):
            cols = slice(h * DH, (h + 1) * DH)
            before = acc[h]
            pre_ref[b, h] = hi_lo(before)
            acc[h] = before + lax.dot_general(
                k_ref[rows, cols], v_ref[rows, cols], (((0,), (0,)), ((), ())),
                preferred_element_type=F32,
            )

    @pl.when(step == steps - 1)
    def _():
        tot_ref[...] = acc[...]


def project(x, w_qkv, tile=512):
    tokens, width = x.shape
    feats = w_qkv.shape[2]
    heads = feats // DH
    blocks = tile // BLK
    rows = pl.BlockSpec((tile, feats), lambda i: (i, 0))
    return pl.pallas_call(
        qkv_kernel,
        grid=(tokens // tile,),
        in_specs=[pl.BlockSpec(memory_space=pl.ANY)] * 2,
        out_specs=[
            rows,
            rows,
            rows,
            pl.BlockSpec((blocks, heads, 2 * DH, DH), lambda i: (i, 0, 0, 0)),
            pl.BlockSpec((heads, DH, DH), lambda i: (0, 0, 0)),
        ],
        out_shape=[jax.ShapeDtypeStruct((tokens, feats), BF16)] * 3
        + [
            jax.ShapeDtypeStruct((tokens // BLK, heads, 2 * DH, DH), BF16),
            jax.ShapeDtypeStruct((heads, DH, DH), F32),
        ],
        scratch_shapes=[
            pltpu.VMEM((heads, DH, DH), F32),
            pltpu.VMEM((2, tile, width), BF16),
            pltpu.VMEM((3, width, feats), BF16),
            pltpu.SemaphoreType.DMA((2,)),
            pltpu.SemaphoreType.DMA((3,)),
        ],
        cost_estimate=cost(6 * tokens * width * feats, 2 * tokens * width + 6 * width * feats),
        name="project",
    )(x, w_qkv)


def local_kernel(q_ref, k_ref, v_ref, pre_ref, *rest):
    att_ref = rest[-1]
    heads = pre_ref.shape[1]
    lower = lax.broadcasted_iota(jnp.int32, (BLK, BLK), 0) >= lax.broadcasted_iota(
        jnp.int32, (BLK, BLK), 1
    )
    for b in range(q_ref.shape[0] // BLK):
        rows = slice(b * BLK, (b + 1) * BLK)
        for h in range(heads):
            cols = slice(h * DH, (h + 1) * DH)
            q = q_ref[rows, cols]
            scores = lax.dot_general(
                q, k_ref[rows, cols], (((1,), (1,)), ((), ())), preferred_element_type=F32
            )
            scores = jnp.where(lower, scores, 0.0).astype(BF16)
            att_ref[rows, cols] = dot(scores, v_ref[rows, cols]) + dot(
                jnp.concatenate([q, q], axis=1), pre_ref[b, h]
            )


def local_part(q, k, v, pre, att, piece, pieces, tile=256):
    tokens, feats = q.shape
    heads = feats // DH
    blocks = tile // BLK
    count = tokens // pieces
    start = piece * count // tile
    row = pl.BlockSpec((tile, feats), lambda i: (i + start, 0))
    return pl.pallas_call(
        local_kernel,
        grid=(count // tile,),
        in_specs=[
            row, row, row,
            pl.BlockSpec((blocks, heads, 2 * DH, DH), lambda i: (i + start, 0, 0, 0)),
        ]
        + [pl.BlockSpec(memory_space=pl.ANY)] * len(att),
        out_specs=row,
        out_shape=jax.ShapeDtypeStruct((tokens, feats), F32),
        input_output_aliases={4: 0} if att else {},
        cost_estimate=cost(8 * count * feats * BLK, 14 * count * feats),
        name="local_part",
    )(q, k, v, pre, *att)


def finish_kernel(place, q_ref, att_ref, core_ref, y1_ref, y2_ref, x1_ref, x2_ref, gain_ref, n_ref):
    heads = core_ref.shape[0]
    core, y, x = place[1], place[2], place[3]
    takes = (
        (core == 1, core_ref),
        (lax.rem(y, 2) == 1, y1_ref),
        (y >= 2, y2_ref),
        (lax.rem(x, 2) == 1, x1_ref),
        (x >= 2, x2_ref),
    )
    for h in range(heads):
        cols = slice(h * DH, (h + 1) * DH)
        carried = jnp.zeros((DH, DH), F32)
        for take, ref in takes:
            carried = carried + jnp.where(take, ref[h].astype(F32), 0.0)
        q = q_ref[:, cols]
        att = att_ref[:, cols] + dot(jnp.concatenate([q, q], axis=1), hi_lo(carried))
        mean_sq = jnp.mean(att * att, axis=-1, keepdims=True)
        n_ref[:, cols] = (att / jnp.sqrt(mean_sq + 1e-06) * gain_ref[:, cols]).astype(BF16)


def finish(place, direction, shift, q, att, received, gain, parts, tile=256):
    tokens, feats = q.shape
    count = tokens // parts
    per = count // tile
    heads = feats // DH

    def row(i, place):
        to = place[0] + direction * (1 - 2 * place[1]) + shift + parts
        return (lax.rem(to, parts) * per + i, 0)

    return pl.pallas_call(
        finish_kernel,
        grid_spec=pltpu.PrefetchScalarGridSpec(
            num_scalar_prefetch=1,
            grid=(per,),
            in_specs=[pl.BlockSpec((tile, feats), row), pl.BlockSpec((tile, feats), row)]
            + [pl.BlockSpec((heads, DH, DH), lambda i, place: (0, 0, 0))] * len(received)
            + [pl.BlockSpec((1, feats), lambda i, place: (0, 0))],
            out_specs=pl.BlockSpec((tile, feats), lambda i, place: (i, 0)),
        ),
        out_shape=jax.ShapeDtypeStruct((count, feats), BF16),
        cost_estimate=cost(2 * count * feats * DH * 2, count * feats * 8),
        name="finish",
    )(place, q, att, *received, gain)


def first_kernel(n0, na, w0, wa, acc_ref):
    acc_ref[...] = dot(n0[...], w0[...]) + dot(na[...], wa[...])


def last_kernel(core, acc_ref, nb, nf, wb, mine_ref, other_ref, out_ref):
    half = mine_ref.shape[0]
    mine = pl.multiple_of(core[0] * half, half)
    other = pl.multiple_of((1 - core[0]) * half, half)
    acc = acc_ref[...] + dot(nb[...], wb[...])
    acc += dot(nf[:, pl.ds(mine, half)], mine_ref[...])
    acc += dot(nf[:, pl.ds(other, half)], other_ref[...])
    out_ref[...] = acc.astype(BF16)


def mix_first(normed, weights, tile=512):
    rows, feats = normed[0].shape
    width = weights[0].shape[1]
    return pl.pallas_call(
        first_kernel,
        grid=(width // tile,),
        in_specs=[pl.BlockSpec(a.shape, lambda i: (0, 0)) for a in normed]
        + [pl.BlockSpec((a.shape[0], tile), lambda i: (0, i)) for a in weights],
        out_specs=pl.BlockSpec((rows, tile), lambda i: (0, i)),
        out_shape=jax.ShapeDtypeStruct((rows, width), F32),
        cost_estimate=cost(4 * rows * feats * width, 8 * rows * width),
        compiler_params=pltpu.CompilerParams(vmem_limit_bytes=24 << 20),
        name="mix_first",
    )(*normed, *weights)


def mix_last(core, acc, normed, weights, tile=512):
    rows, feats = normed[0].shape
    width = acc.shape[1]
    column = lambda a: pl.BlockSpec((a.shape[0], tile), lambda i, core: (0, i))
    return pl.pallas_call(
        last_kernel,
        grid_spec=pltpu.PrefetchScalarGridSpec(
            num_scalar_prefetch=1,
            grid=(width // tile,),
            in_specs=[column(acc)]
            + [pl.BlockSpec(a.shape, lambda i, core: (0, 0)) for a in normed]
            + [column(a) for a in weights],
            out_specs=pl.BlockSpec((rows, tile), lambda i, core: (0, i)),
        ),
        out_shape=jax.ShapeDtypeStruct((rows, width), BF16),
        cost_estimate=cost(4 * rows * feats * width, 8 * rows * width),
        compiler_params=pltpu.CompilerParams(vmem_limit_bytes=24 << 20),
        name="mix_last",
    )(core, acc, *normed, *weights)


def pair_up(size, stride, total, first):
    pairs = []
    for i in range(total):
        at = (i // stride) % size
        to = at ^ 1 if first else (at + (1 if at % 2 else -1)) % size
        pairs.append((i, i + (to - at) * stride))
    return pairs


def pair_rounds(value, stride, total):
    value = value.astype(BF16)
    other = lax.ppermute(value, "seq", pair_up(4, stride, total, True))
    pair = (value.astype(F32) + other.astype(F32)).astype(BF16)
    far = lax.ppermute(pair, "seq", pair_up(4, stride, total, False))
    return other, far, pair.astype(F32) + far.astype(F32)


def layer(inputs, w_qkv, norm_gain, w_out):
    parts = lax.axis_size("head")
    total = lax.axis_size("seq")
    seq = lax.axis_index("seq")
    core = lax.rem(seq, 2)
    y = lax.rem(seq // 2, 4)
    x = seq // 8
    head = lax.axis_index("head")
    core_id = core.astype(jnp.int32).reshape(1)
    place = jnp.stack([head, core, y, x]).astype(jnp.int32)

    def along(direction):
        pairs = []
        for i in range(total):
            shift = direction * (1 - 2 * (i % 2))
            for h in range(parts):
                pairs.append((i * parts + h, i * parts + (h + shift) % parts))
        return pairs

    partner = [(i, i ^ 1) for i in range(total)]

    def swap(a):
        return lax.ppermute(a, "seq", partner)

    def send(a, direction):
        return lax.ppermute(a, ("seq", "head"), along(direction))

    near = send(w_out, 1)
    rows = w_out.shape[0] // 2
    far = send(lax.dynamic_slice_in_dim(near, core * rows, rows, 0), 1)
    near_other = swap(near)
    far_other = swap(far)

    q, k, v, pre, tot = project(inputs, w_qkv)
    other = swap(tot)
    att = []
    for piece in range(4):
        att = [local_part(q, k, v, pre, att, piece, 4)]
    att = att[0]
    y1, y2, row = pair_rounds(tot + other, 2, total)
    x1, x2, _ = pair_rounds(row, 8, total)
    received = (other, y1, y2, x1, x2)

    gain = norm_gain.reshape(1, -1)
    nf = send(finish(place, 0, 2, q, att, received, gain, parts), 1)
    na = send(finish(place, 1, 0, q, att, received, gain, parts), 1)
    nb = send(finish(place, -1, 0, q, att, received, gain, parts), -1)
    nf = send(nf, 1)
    n0 = finish(place, 0, 0, q, att, received, gain, parts)
    acc = mix_first([n0, na], [w_out, near])
    return mix_last(core_id, acc, [nb, nf], [near_other, far, far_other])


def solution(mesh):
    return jax.shard_map(
        layer,
        mesh=mesh,
        in_specs=(P("seq", None), P(None, None, "head"), P("head"), P("head", None)),
        out_specs=P(("seq", "head"), None),
        check_vma=False,
    )
```

```python
import jax
import jax.numpy as jnp
from jax import lax
from jax.experimental import pallas as pl
from jax.experimental.pallas import tpu as pltpu
from jax.sharding import PartitionSpec as P


DH = 128
BLK = 256
F32 = jnp.float32
BF16 = jnp.bfloat16


def dot(a, b):
    return jnp.dot(a, b, preferred_element_type=F32)


def cost(flops, nbytes):
    return pl.CostEstimate(flops=int(flops), bytes_accessed=int(nbytes), transcendentals=0)


def hi_lo(state):
    high = state.astype(BF16)
    low = (state - high.astype(F32)).astype(BF16)
    return jnp.concatenate([high, low], axis=0)


def local_block(att_ref, rows, q_ref, k_ref, v_ref, pre, at):
    lower = lax.broadcasted_iota(jnp.int32, (BLK, BLK), 0) >= lax.broadcasted_iota(
        jnp.int32, (BLK, BLK), 1
    )
    for h in range(q_ref.shape[1] // DH):
        cols = slice(h * DH, (h + 1) * DH)
        q = q_ref[rows, cols]
        scores = lax.dot_general(
            q, k_ref[rows, cols], (((1,), (1,)), ((), ())), preferred_element_type=F32
        )
        scores = jnp.where(lower, scores, 0.0).astype(BF16)
        left = jnp.concatenate([scores, q, q], axis=1)
        right = jnp.concatenate([v_ref[rows, cols], pre[at, h]], axis=0)
        att_ref[rows, cols] = dot(left, right)


def qkv_kernel(
    x_hbm, w_hbm, q_hbm, k_hbm, v_hbm, pre_hbm, tot_ref, att_hbm,
    x, w, q, k, v, pre, att, x_sem, w_sem, out_sem,
):
    steps = x_sem.shape[0] // 2
    tile = x.shape[0] // steps
    width = x.shape[1]
    half = width // 2
    heads = tot_ref.shape[0]
    blocks = tile // BLK
    inside = att.shape[0] // tile

    def tokens(i, part):
        at = (pl.ds(i * tile, tile), pl.ds(part * half, half))
        return pltpu.make_async_copy(x_hbm.at[at], x.at[at], x_sem.at[2 * i + part])

    def weight(which, part):
        at = pl.ds(part * half, half)
        return pltpu.make_async_copy(
            w_hbm.at[which, at], w.at[which, at], w_sem.at[2 * which + part]
        )

    for part in range(2):
        tokens(0, part).start()
        weight(1, part).start()
    for which in (2, 0):
        for part in range(2):
            weight(which, part).start()
    for i in range(1, steps):
        for part in range(2):
            tokens(i, part).start()

    pending = []

    def put(i, source, target, which):
        copy = pltpu.make_async_copy(source, target, out_sem.at[i, which])
        copy.start()
        pending.append(copy)

    state = [jnp.zeros((DH, DH), F32)] * heads
    for i in range(steps):
        rows = pl.ds(i * tile, tile)
        if i == 0:
            total = None
            for part in range(2):
                tokens(0, part).wait()
                weight(1, part).wait()
                cut = pl.ds(part * half, half)
                product = dot(x[rows, cut], w[1, cut])
                total = product if total is None else total + product
            k[rows] = total.astype(BF16)
        else:
            for part in range(2):
                tokens(i, part).wait()
            k[rows] = dot(x[rows], w[1]).astype(BF16)
        for which, out in ((2, v), (0, q)):
            if i == 0:
                for part in range(2):
                    weight(which, part).wait()
            out[rows] = dot(x[rows], w[which]).astype(BF16)
        for b in range(i * blocks, (i + 1) * blocks):
            block = slice(b * BLK, (b + 1) * BLK)
            for h in range(heads):
                cols = slice(h * DH, (h + 1) * DH)
                pre[b, h] = hi_lo(state[h])
                state[h] = state[h] + lax.dot_general(
                    k[block, cols], v[block, cols], (((0,), (0,)), ((), ())),
                    preferred_element_type=F32,
                )
            if i < inside:
                local_block(att, block, q, k, v, pre, b)
        put(i, q.at[rows], q_hbm.at[rows], 0)
        put(i, k.at[rows], k_hbm.at[rows], 1)
        put(i, v.at[rows], v_hbm.at[rows], 2)
        at = pl.ds(i * blocks, blocks)
        put(i, pre.at[at], pre_hbm.at[at], 3)
        if i < inside:
            put(i, att.at[rows], att_hbm.at[rows], 4)
    for h in range(heads):
        tot_ref[h] = state[h]
    for copy in pending:
        copy.wait()


def project(x, w_qkv, inside, tile=512):
    tokens, width = x.shape
    feats = w_qkv.shape[2]
    heads = feats // DH
    steps = tokens // tile
    wide = (tokens, feats)
    states = (tokens // BLK, heads, 2 * DH, DH)
    anywhere = pl.BlockSpec(memory_space=pl.ANY)
    return pl.pallas_call(
        qkv_kernel,
        in_specs=[anywhere] * 2,
        out_specs=[anywhere] * 4 + [pl.BlockSpec(memory_space=pltpu.VMEM), anywhere],
        out_shape=[jax.ShapeDtypeStruct(wide, BF16)] * 3
        + [
            jax.ShapeDtypeStruct(states, BF16),
            jax.ShapeDtypeStruct((heads, DH, DH), F32),
            jax.ShapeDtypeStruct(wide, F32),
        ],
        scratch_shapes=[
            pltpu.VMEM((tokens, width), BF16),
            pltpu.VMEM((3, width, feats), BF16),
            pltpu.VMEM(wide, BF16),
            pltpu.VMEM(wide, BF16),
            pltpu.VMEM(wide, BF16),
            pltpu.VMEM(states, BF16),
            pltpu.VMEM((inside * tile, feats), F32),
            pltpu.SemaphoreType.DMA((2 * steps,)),
            pltpu.SemaphoreType.DMA((6,)),
            pltpu.SemaphoreType.DMA((steps, 5)),
        ],
        cost_estimate=cost(6 * tokens * width * feats, 2 * tokens * width + 6 * width * feats),
        name="project",
    )(x, w_qkv)


def local_kernel(q_ref, k_ref, v_ref, pre_ref, att_in, att_ref):
    for b in range(q_ref.shape[0] // BLK):
        local_block(att_ref, slice(b * BLK, (b + 1) * BLK), q_ref, k_ref, v_ref, pre_ref, b)


def local_part(q, k, v, pre, att, piece, pieces, tile=256):
    tokens, feats = q.shape
    heads = feats // DH
    blocks = tile // BLK
    count = tokens // pieces
    start = piece * count // tile
    row = pl.BlockSpec((tile, feats), lambda i: (i + start, 0))
    return pl.pallas_call(
        local_kernel,
        grid=(count // tile,),
        in_specs=[
            row, row, row,
            pl.BlockSpec((blocks, heads, 2 * DH, DH), lambda i: (i + start, 0, 0, 0)),
            pl.BlockSpec(memory_space=pl.ANY),
        ],
        out_specs=row,
        out_shape=jax.ShapeDtypeStruct((tokens, feats), F32),
        input_output_aliases={4: 0},
        cost_estimate=cost(8 * count * feats * BLK, 14 * count * feats),
        name="local_part",
    )(q, k, v, pre, att)


def norm_rows(q_ref, att_ref, pair, gain_ref, n_ref, h):
    cols = slice(h * DH, (h + 1) * DH)
    q = q_ref[:, cols]
    att = att_ref[:, cols] + dot(jnp.concatenate([q, q], axis=1), pair)
    mean_sq = jnp.mean(att * att, axis=-1, keepdims=True)
    n_ref[:, cols] = (att * lax.rsqrt(mean_sq + 1e-06) * gain_ref[:, cols]).astype(BF16)


def start_kernel(
    head, core, y, x, q_ref, att_ref, core_ref, y1_ref, y2_ref, x1_ref, x2_ref, gain_ref,
    n_ref, pair_ref,
):
    takes = (
        (core[0] == 1, core_ref),
        (lax.rem(y[0], 2) == 1, y1_ref),
        (y[0] >= 2, y2_ref),
        (lax.rem(x[0], 2) == 1, x1_ref),
        (x[0] >= 2, x2_ref),
    )
    for h in range(core_ref.shape[0]):

        @pl.when(pl.program_id(0) == 0)
        def _():
            carried = jnp.zeros((DH, DH), F32)
            for take, ref in takes:
                carried = carried + jnp.where(take, ref[h].astype(F32), 0.0)
            pair_ref[h] = hi_lo(carried)

    for h in range(core_ref.shape[0]):
        norm_rows(q_ref, att_ref, pair_ref[h], gain_ref, n_ref, h)


def finish_kernel(head, core, y, x, q_ref, att_ref, pair_ref, gain_ref, n_ref):
    for h in range(pair_ref.shape[0]):
        norm_rows(q_ref, att_ref, pair_ref[h], gain_ref, n_ref, h)


def finish(place, direction, shift, q, att, received, gain, parts, tile=256):
    tokens, feats = q.shape
    count = tokens // parts
    per = count // tile
    heads = feats // DH

    def row(i, head, core, y, x):
        to = head[0] + direction * (1 - 2 * core[0]) + shift + parts
        return (lax.rem(to, parts) * per + i, 0)

    first = len(received) > 1
    normed = jax.ShapeDtypeStruct((count, feats), BF16)
    rows = pl.BlockSpec((tile, feats), lambda i, *place: (i, 0))
    whole = lambda a: pl.BlockSpec(a.shape, lambda i, *place: (0,) * len(a.shape))
    pair = jax.ShapeDtypeStruct((heads, 2 * DH, DH), BF16)
    return pl.pallas_call(
        start_kernel if first else finish_kernel,
        grid_spec=pltpu.PrefetchScalarGridSpec(
            num_scalar_prefetch=4,
            grid=(per,),
            in_specs=[pl.BlockSpec((tile, feats), row), pl.BlockSpec((tile, feats), row)]
            + [whole(a) for a in received]
            + [whole(gain)],
            out_specs=[rows, whole(pair)] if first else rows,
        ),
        out_shape=[normed, pair] if first else normed,
        cost_estimate=cost(2 * count * feats * DH * 2, count * feats * 8),
        name="finish",
    )(*place, q, att, *received, gain)


def first_kernel(n0, na, w0, wa, *rest):
    acc_ref = rest[-1]
    acc_ref[...] = dot(n0[...], w0[...]) + dot(na[...], wa[...])


def last_kernel(
    core, acc_hbm, nb_hbm, nf_hbm, wb_hbm, mine_hbm, other_hbm, out_hbm,
    acc, nb, nf, wb, mine, other, out, n_sem, w_sem, out_sem,
):
    tiles = w_sem.shape[0]
    tile = out.shape[1] // tiles
    half = mine.shape[0]
    rows = [pltpu.make_async_copy(nb_hbm, nb, n_sem.at[0]), pltpu.make_async_copy(nf_hbm, nf, n_sem.at[1])]
    columns = [slice(j * tile, (j + 1) * tile) for j in range(tiles)]
    weights = [
        [
            pltpu.make_async_copy(source.at[:, cut], target.at[:, cut], w_sem.at[j, which])
            for which, (source, target) in enumerate(
                ((wb_hbm, wb), (mine_hbm, mine), (other_hbm, other), (acc_hbm, acc))
            )
        ]
        for j, cut in enumerate(columns)
    ]
    for which in range(2):
        rows[which].start()
        for copy in weights[0][which :: 2]:
            copy.start()
    for copies in weights[1:]:
        for copy in copies:
            copy.start()
    own = pl.multiple_of(core[0] * half, half)
    partner = pl.multiple_of((1 - core[0]) * half, half)
    pending = []
    for j, cut in enumerate(columns):
        if j == 0:
            rows[0].wait()
        weights[j][0].wait()
        total = dot(nb[...], wb[:, cut])
        if j == 0:
            rows[1].wait()
        weights[j][1].wait()
        total += dot(nf[:, pl.ds(own, half)], mine[:, cut])
        weights[j][2].wait()
        total += dot(nf[:, pl.ds(partner, half)], other[:, cut])
        weights[j][3].wait()
        out[:, cut] = (total + acc[:, cut]).astype(BF16)
        copy = pltpu.make_async_copy(out.at[:, cut], out_hbm.at[:, cut], out_sem.at[j])
        copy.start()
        pending.append(copy)
    for copy in pending:
        copy.wait()


def mix_first(normed, weights, later, tile=512):
    rows, feats = normed[0].shape
    width = weights[0].shape[1]
    return pl.pallas_call(
        first_kernel,
        grid=(width // tile,),
        in_specs=[pl.BlockSpec(a.shape, lambda i: (0, 0)) for a in normed]
        + [pl.BlockSpec((a.shape[0], tile), lambda i: (0, i)) for a in weights]
        + [pl.BlockSpec(memory_space=pl.ANY)] * len(later),
        out_specs=pl.BlockSpec((rows, tile), lambda i: (0, i)),
        out_shape=jax.ShapeDtypeStruct((rows, width), F32),
        cost_estimate=cost(4 * rows * feats * width, 8 * rows * width),
        compiler_params=pltpu.CompilerParams(vmem_limit_bytes=24 << 20),
        name="mix_first",
    )(*normed, *weights, *later)


def mix_last(core, acc, normed, weights, tiles=2):
    rows, feats = normed[0].shape
    width = acc.shape[1]
    anywhere = pl.BlockSpec(memory_space=pl.ANY)
    operands = [acc, *normed, *weights]
    return pl.pallas_call(
        last_kernel,
        grid_spec=pltpu.PrefetchScalarGridSpec(
            num_scalar_prefetch=1,
            grid=(1,),
            in_specs=[anywhere] * len(operands),
            out_specs=anywhere,
            scratch_shapes=[pltpu.VMEM(a.shape, a.dtype) for a in operands]
            + [
                pltpu.VMEM((rows, width), BF16),
                pltpu.SemaphoreType.DMA((2,)),
                pltpu.SemaphoreType.DMA((tiles, 4)),
                pltpu.SemaphoreType.DMA((tiles,)),
            ],
        ),
        out_shape=jax.ShapeDtypeStruct((rows, width), BF16),
        cost_estimate=cost(4 * rows * feats * width, 8 * rows * width),
        compiler_params=pltpu.CompilerParams(vmem_limit_bytes=24 << 20),
        name="mix_last",
    )(core, *operands)


def pair_up(size, stride, total, first):
    pairs = []
    for i in range(total):
        at = (i // stride) % size
        to = at ^ 1 if first else (at + (1 if at % 2 else -1)) % size
        pairs.append((i, i + (to - at) * stride))
    return pairs


def pair_rounds(value, stride, total):
    value = value.astype(BF16)
    other = lax.ppermute(value, "seq", pair_up(4, stride, total, True))
    pair = (value.astype(F32) + other.astype(F32)).astype(BF16)
    far = lax.ppermute(pair, "seq", pair_up(4, stride, total, False))
    return other, far, pair.astype(F32) + far.astype(F32)


def layer(inputs, w_qkv, norm_gain, w_out):
    parts = lax.axis_size("head")
    total = lax.axis_size("seq")
    seq = lax.axis_index("seq")
    core = lax.rem(seq, 2)
    y = lax.rem(seq // 2, 4)
    x = seq // 8
    head = lax.axis_index("head")
    core_id = core.astype(jnp.int32).reshape(1)
    place = [a.astype(jnp.int32).reshape(1) for a in (head, core, y, x)]

    def along(direction):
        pairs = []
        for i in range(total):
            shift = direction * (1 - 2 * (i % 2))
            for h in range(parts):
                pairs.append((i * parts + h, i * parts + (h + shift) % parts))
        return pairs

    partner = [(i, i ^ 1) for i in range(total)]

    def swap(a):
        return lax.ppermute(a, "seq", partner)

    def send(a, direction):
        return lax.ppermute(a, ("seq", "head"), along(direction))

    near = send(w_out, 1)
    rows = w_out.shape[0] // 2
    far = lax.dynamic_slice_in_dim(near, core * rows, rows, 0)
    far = send(far, 1)
    near_other = swap(near)
    far_other = swap(far)

    q, k, v, pre, tot, att = project(inputs, w_qkv, 1)
    other = swap(tot)
    for piece in range(1, 4):
        att = local_part(q, k, v, pre, att, piece, 4)
    y1, y2, row = pair_rounds(tot + other, 2, total)
    x1, x2, _ = pair_rounds(row, 8, total)
    received = (other, y1, y2, x1, x2)

    gain = norm_gain.reshape(1, -1)
    nf, pair = finish(place, 0, 2, q, att, received, gain, parts)
    nf = send(nf, 1)
    na = send(finish(place, 1, 0, q, att, (pair,), gain, parts), 1)
    nb = send(finish(place, -1, 0, q, att, (pair,), gain, parts), -1)
    nf = send(nf, 1)
    n0 = finish(place, 0, 0, q, att, (pair,), gain, parts)
    later = [near_other, far, far_other]
    acc = mix_first([n0, na], [w_out, near], later)
    return mix_last(core_id, acc, [nb, nf], later)


def solution(mesh):
    return jax.shard_map(
        layer,
        mesh=mesh,
        in_specs=(P("seq", None), P(None, None, "head"), P("head"), P("head", None)),
        out_specs=P(("seq", "head"), None),
        check_vma=False,
    )
```

```python
import jax
import jax.numpy as jnp
from jax import lax
from jax.experimental import pallas as pl
from jax.experimental.pallas import tpu as pltpu
from jax.sharding import PartitionSpec as P


DH = 128
BLK = 256
F32 = jnp.float32
BF16 = jnp.bfloat16


def dot(a, b):
    return jnp.dot(a, b, preferred_element_type=F32)


def cost(flops, nbytes):
    return pl.CostEstimate(flops=int(flops), bytes_accessed=int(nbytes), transcendentals=0)


def hi_lo(state):
    high = state.astype(BF16)
    low = (state - high.astype(F32)).astype(BF16)
    return jnp.concatenate([high, low], axis=0)


def local_block(att_ref, rows, q_ref, k_ref, v_ref, pre, at):
    lower = lax.broadcasted_iota(jnp.int32, (BLK, BLK), 0) >= lax.broadcasted_iota(
        jnp.int32, (BLK, BLK), 1
    )
    for h in range(q_ref.shape[1] // DH):
        cols = slice(h * DH, (h + 1) * DH)
        q = q_ref[rows, cols]
        scores = lax.dot_general(
            q, k_ref[rows, cols], (((1,), (1,)), ((), ())), preferred_element_type=F32
        )
        scores = jnp.where(lower, scores, 0.0).astype(BF16)
        att_ref[rows, cols] = dot(scores, v_ref[rows, cols]) + dot(
            jnp.concatenate([q, q], axis=1), pre[at, h]
        )


def qkv_kernel(
    x_hbm, w_hbm, q_hbm, k_hbm, v_hbm, pre_hbm, tot_ref, att_hbm,
    x, w, q, k, v, pre, att, x_sem, w_sem, out_sem,
):
    steps = x_sem.shape[0] // 2
    tile = x.shape[0] // steps
    width = x.shape[1]
    half = width // 2
    heads = tot_ref.shape[0]
    blocks = tile // BLK
    inside = att.shape[0] // tile

    def tokens(i, part):
        at = (pl.ds(i * tile, tile), pl.ds(part * half, half))
        return pltpu.make_async_copy(x_hbm.at[at], x.at[at], x_sem.at[2 * i + part])

    def weight(which, part):
        at = pl.ds(part * half, half)
        return pltpu.make_async_copy(
            w_hbm.at[which, at], w.at[which, at], w_sem.at[2 * which + part]
        )

    for part in range(2):
        tokens(0, part).start()
        weight(1, part).start()
    for which in (2, 0):
        for part in range(2):
            weight(which, part).start()
    for i in range(1, steps):
        for part in range(2):
            tokens(i, part).start()

    pending = []

    def put(i, source, target, which):
        copy = pltpu.make_async_copy(source, target, out_sem.at[i, which])
        copy.start()
        pending.append(copy)

    state = [jnp.zeros((DH, DH), F32)] * heads
    for i in range(steps):
        rows = pl.ds(i * tile, tile)
        if i == 0:
            total = None
            for part in range(2):
                tokens(0, part).wait()
                weight(1, part).wait()
                cut = pl.ds(part * half, half)
                product = dot(x[rows, cut], w[1, cut])
                total = product if total is None else total + product
            k[rows] = total.astype(BF16)
        else:
            for part in range(2):
                tokens(i, part).wait()
            k[rows] = dot(x[rows], w[1]).astype(BF16)
        for which, out in ((2, v), (0, q)):
            if i == 0:
                for part in range(2):
                    weight(which, part).wait()
            out[rows] = dot(x[rows], w[which]).astype(BF16)
        for b in range(i * blocks, (i + 1) * blocks):
            block = slice(b * BLK, (b + 1) * BLK)
            for h in range(heads):
                cols = slice(h * DH, (h + 1) * DH)
                pre[b, h] = hi_lo(state[h])
                state[h] = state[h] + lax.dot_general(
                    k[block, cols], v[block, cols], (((0,), (0,)), ((), ())),
                    preferred_element_type=F32,
                )
            if i < inside:
                local_block(att, block, q, k, v, pre, b)
        put(i, q.at[rows], q_hbm.at[rows], 0)
        put(i, k.at[rows], k_hbm.at[rows], 1)
        put(i, v.at[rows], v_hbm.at[rows], 2)
        at = pl.ds(i * blocks, blocks)
        put(i, pre.at[at], pre_hbm.at[at], 3)
        if i < inside:
            put(i, att.at[rows], att_hbm.at[rows], 4)
    for h in range(heads):
        tot_ref[h] = state[h]
    for copy in pending:
        copy.wait()


def project(x, w_qkv, inside, tile=512):
    tokens, width = x.shape
    feats = w_qkv.shape[2]
    heads = feats // DH
    steps = tokens // tile
    wide = (tokens, feats)
    states = (tokens // BLK, heads, 2 * DH, DH)
    anywhere = pl.BlockSpec(memory_space=pl.ANY)
    return pl.pallas_call(
        qkv_kernel,
        in_specs=[anywhere] * 2,
        out_specs=[anywhere] * 4 + [pl.BlockSpec(memory_space=pltpu.VMEM), anywhere],
        out_shape=[jax.ShapeDtypeStruct(wide, BF16)] * 3
        + [
            jax.ShapeDtypeStruct(states, BF16),
            jax.ShapeDtypeStruct((heads, DH, DH), F32),
            jax.ShapeDtypeStruct(wide, F32),
        ],
        scratch_shapes=[
            pltpu.VMEM((tokens, width), BF16),
            pltpu.VMEM((3, width, feats), BF16),
            pltpu.VMEM(wide, BF16),
            pltpu.VMEM(wide, BF16),
            pltpu.VMEM(wide, BF16),
            pltpu.VMEM(states, BF16),
            pltpu.VMEM((inside * tile, feats), F32),
            pltpu.SemaphoreType.DMA((2 * steps,)),
            pltpu.SemaphoreType.DMA((6,)),
            pltpu.SemaphoreType.DMA((steps, 5)),
        ],
        cost_estimate=cost(6 * tokens * width * feats, 2 * tokens * width + 6 * width * feats),
        name="project",
    )(x, w_qkv)


def local_kernel(q_ref, k_ref, v_ref, pre_ref, att_in, att_ref):
    for b in range(q_ref.shape[0] // BLK):
        local_block(att_ref, slice(b * BLK, (b + 1) * BLK), q_ref, k_ref, v_ref, pre_ref, b)


def local_part(q, k, v, pre, att, piece, pieces, tile=256):
    tokens, feats = q.shape
    heads = feats // DH
    blocks = tile // BLK
    count = tokens // pieces
    start = piece * count // tile
    row = pl.BlockSpec((tile, feats), lambda i: (i + start, 0))
    return pl.pallas_call(
        local_kernel,
        grid=(count // tile,),
        in_specs=[
            row, row, row,
            pl.BlockSpec((blocks, heads, 2 * DH, DH), lambda i: (i + start, 0, 0, 0)),
            pl.BlockSpec(memory_space=pl.ANY),
        ],
        out_specs=row,
        out_shape=jax.ShapeDtypeStruct((tokens, feats), F32),
        input_output_aliases={4: 0},
        cost_estimate=cost(8 * count * feats * BLK, 14 * count * feats),
        name="local_part",
    )(q, k, v, pre, att)


def norm_rows(q_ref, att_ref, pair, gain_ref, n_ref, h):
    cols = slice(h * DH, (h + 1) * DH)
    q = q_ref[:, cols]
    att = att_ref[:, cols] + dot(jnp.concatenate([q, q], axis=1), pair)
    mean_sq = jnp.mean(att * att, axis=-1, keepdims=True)
    n_ref[:, cols] = (att * lax.rsqrt(mean_sq + 1e-06) * gain_ref[:, cols]).astype(BF16)


def start_kernel(
    head, core, y, x, q_ref, att_ref, core_ref, y1_ref, y2_ref, x1_ref, x2_ref, gain_ref,
    n_ref, pair_ref,
):
    takes = (
        (core[0] == 1, core_ref),
        (lax.rem(y[0], 2) == 1, y1_ref),
        (y[0] >= 2, y2_ref),
        (lax.rem(x[0], 2) == 1, x1_ref),
        (x[0] >= 2, x2_ref),
    )
    for h in range(core_ref.shape[0]):

        @pl.when(pl.program_id(0) == 0)
        def _():
            carried = jnp.zeros((DH, DH), F32)
            for take, ref in takes:
                carried = carried + jnp.where(take, ref[h].astype(F32), 0.0)
            pair_ref[h] = hi_lo(carried)

    for h in range(core_ref.shape[0]):
        norm_rows(q_ref, att_ref, pair_ref[h], gain_ref, n_ref, h)


def finish_kernel(head, core, y, x, q_ref, att_ref, pair_ref, gain_ref, n_ref):
    for h in range(pair_ref.shape[0]):
        norm_rows(q_ref, att_ref, pair_ref[h], gain_ref, n_ref, h)


def finish(place, direction, shift, q, att, received, gain, parts, tile=256):
    tokens, feats = q.shape
    count = tokens // parts
    per = count // tile
    heads = feats // DH

    def row(i, head, core, y, x):
        to = head[0] + direction * (1 - 2 * core[0]) + shift + parts
        return (lax.rem(to, parts) * per + i, 0)

    first = len(received) > 1
    normed = jax.ShapeDtypeStruct((count, feats), BF16)
    rows = pl.BlockSpec((tile, feats), lambda i, *place: (i, 0))
    whole = lambda a: pl.BlockSpec(a.shape, lambda i, *place: (0,) * len(a.shape))
    pair = jax.ShapeDtypeStruct((heads, 2 * DH, DH), BF16)
    return pl.pallas_call(
        start_kernel if first else finish_kernel,
        grid_spec=pltpu.PrefetchScalarGridSpec(
            num_scalar_prefetch=4,
            grid=(per,),
            in_specs=[pl.BlockSpec((tile, feats), row), pl.BlockSpec((tile, feats), row)]
            + [whole(a) for a in received]
            + [whole(gain)],
            out_specs=[rows, whole(pair)] if first else rows,
        ),
        out_shape=[normed, pair] if first else normed,
        cost_estimate=cost(2 * count * feats * DH * 2, count * feats * 8),
        name="finish",
    )(*place, q, att, *received, gain)


def first_kernel(n0, na, w0, wa, *rest):
    acc_ref = rest[-1]
    acc_ref[...] = dot(n0[...], w0[...]) + dot(na[...], wa[...])


def last_kernel(
    core, acc_hbm, nb_hbm, nf_hbm, wb_hbm, mine_hbm, other_hbm, out_hbm,
    acc, nb, nf, wb, mine, other, out, n_sem, w_sem, out_sem,
):
    tiles = w_sem.shape[0]
    tile = out.shape[1] // tiles
    half = mine.shape[0]
    rows = [pltpu.make_async_copy(nb_hbm, nb, n_sem.at[0]), pltpu.make_async_copy(nf_hbm, nf, n_sem.at[1])]
    columns = [slice(j * tile, (j + 1) * tile) for j in range(tiles)]
    weights = [
        [
            pltpu.make_async_copy(source.at[:, cut], target.at[:, cut], w_sem.at[j, which])
            for which, (source, target) in enumerate(
                ((wb_hbm, wb), (mine_hbm, mine), (other_hbm, other), (acc_hbm, acc))
            )
        ]
        for j, cut in enumerate(columns)
    ]
    for which in range(2):
        rows[which].start()
        for copy in weights[0][which :: 2]:
            copy.start()
    for copies in weights[1:]:
        for copy in copies:
            copy.start()
    own = pl.multiple_of(core[0] * half, half)
    partner = pl.multiple_of((1 - core[0]) * half, half)
    pending = []
    for j, cut in enumerate(columns):
        if j == 0:
            rows[0].wait()
        weights[j][0].wait()
        total = dot(nb[...], wb[:, cut])
        if j == 0:
            rows[1].wait()
        weights[j][1].wait()
        total += dot(nf[:, pl.ds(own, half)], mine[:, cut])
        weights[j][2].wait()
        total += dot(nf[:, pl.ds(partner, half)], other[:, cut])
        weights[j][3].wait()
        out[:, cut] = (total + acc[:, cut]).astype(BF16)
        copy = pltpu.make_async_copy(out.at[:, cut], out_hbm.at[:, cut], out_sem.at[j])
        copy.start()
        pending.append(copy)
    for copy in pending:
        copy.wait()


def mix_first(normed, weights, later, tile=512):
    rows, feats = normed[0].shape
    width = weights[0].shape[1]
    return pl.pallas_call(
        first_kernel,
        grid=(width // tile,),
        in_specs=[pl.BlockSpec(a.shape, lambda i: (0, 0)) for a in normed]
        + [pl.BlockSpec((a.shape[0], tile), lambda i: (0, i)) for a in weights]
        + [pl.BlockSpec(memory_space=pl.ANY)] * len(later),
        out_specs=pl.BlockSpec((rows, tile), lambda i: (0, i)),
        out_shape=jax.ShapeDtypeStruct((rows, width), F32),
        cost_estimate=cost(4 * rows * feats * width, 8 * rows * width),
        compiler_params=pltpu.CompilerParams(vmem_limit_bytes=24 << 20),
        name="mix_first",
    )(*normed, *weights, *later)


def mix_last(core, acc, normed, weights, tiles=2):
    rows, feats = normed[0].shape
    width = acc.shape[1]
    anywhere = pl.BlockSpec(memory_space=pl.ANY)
    operands = [acc, *normed, *weights]
    return pl.pallas_call(
        last_kernel,
        grid_spec=pltpu.PrefetchScalarGridSpec(
            num_scalar_prefetch=1,
            grid=(1,),
            in_specs=[anywhere] * len(operands),
            out_specs=anywhere,
            scratch_shapes=[pltpu.VMEM(a.shape, a.dtype) for a in operands]
            + [
                pltpu.VMEM((rows, width), BF16),
                pltpu.SemaphoreType.DMA((2,)),
                pltpu.SemaphoreType.DMA((tiles, 4)),
                pltpu.SemaphoreType.DMA((tiles,)),
            ],
        ),
        out_shape=jax.ShapeDtypeStruct((rows, width), BF16),
        cost_estimate=cost(4 * rows * feats * width, 8 * rows * width),
        compiler_params=pltpu.CompilerParams(vmem_limit_bytes=24 << 20),
        name="mix_last",
    )(core, *operands)


def pair_up(size, stride, total, first):
    pairs = []
    for i in range(total):
        at = (i // stride) % size
        to = at ^ 1 if first else (at + (1 if at % 2 else -1)) % size
        pairs.append((i, i + (to - at) * stride))
    return pairs


def pair_rounds(value, stride, total):
    value = value.astype(BF16)
    other = lax.ppermute(value, "seq", pair_up(4, stride, total, True))
    pair = (value.astype(F32) + other.astype(F32)).astype(BF16)
    far = lax.ppermute(pair, "seq", pair_up(4, stride, total, False))
    return other, far, pair.astype(F32) + far.astype(F32)


def layer(inputs, w_qkv, norm_gain, w_out):
    parts = lax.axis_size("head")
    total = lax.axis_size("seq")
    seq = lax.axis_index("seq")
    core = lax.rem(seq, 2)
    y = lax.rem(seq // 2, 4)
    x = seq // 8
    head = lax.axis_index("head")
    core_id = core.astype(jnp.int32).reshape(1)
    place = [a.astype(jnp.int32).reshape(1) for a in (head, core, y, x)]

    def along(direction):
        pairs = []
        for i in range(total):
            shift = direction * (1 - 2 * (i % 2))
            for h in range(parts):
                pairs.append((i * parts + h, i * parts + (h + shift) % parts))
        return pairs

    partner = [(i, i ^ 1) for i in range(total)]

    def swap(a):
        return lax.ppermute(a, "seq", partner)

    def send(a, direction):
        return lax.ppermute(a, ("seq", "head"), along(direction))

    near = send(w_out, 1)
    rows = w_out.shape[0] // 2
    far = lax.dynamic_slice_in_dim(near, core * rows, rows, 0)
    far = send(far, 1)
    near_other = swap(near)
    far_other = swap(far)

    q, k, v, pre, tot, att = project(inputs, w_qkv, 1)
    other = swap(tot)
    for piece in range(1, 4):
        att = local_part(q, k, v, pre, att, piece, 4)
    y1, y2, row = pair_rounds(tot + other, 2, total)
    x1, x2, _ = pair_rounds(row, 8, total)
    received = (other, y1, y2, x1, x2)

    gain = norm_gain.reshape(1, -1)
    na, pair = finish(place, 1, 0, q, att, received, gain, parts)
    na = send(na, 1)
    nf = send(finish(place, 0, 2, q, att, (pair,), gain, parts), 1)
    nb = send(finish(place, -1, 0, q, att, (pair,), gain, parts), -1)
    nf = send(nf, 1)
    n0 = finish(place, 0, 0, q, att, (pair,), gain, parts)
    later = [near_other, far, far_other]
    acc = mix_first([n0, na], [w_out, near], later)
    return mix_last(core_id, acc, [nb, nf], later)


def solution(mesh):
    return jax.shard_map(
        layer,
        mesh=mesh,
        in_specs=(P("seq", None), P(None, None, "head"), P("head"), P("head", None)),
        out_specs=P(("seq", "head"), None),
        check_vma=False,
    )
```

```python
import jax
import jax.numpy as jnp
from jax import lax
from jax.experimental import pallas as pl
from jax.experimental.pallas import tpu as pltpu
from jax.sharding import PartitionSpec as P


DH = 128
BLK = 256
F32 = jnp.float32
BF16 = jnp.bfloat16


def dot(a, b):
    return jnp.dot(a, b, preferred_element_type=F32)


def cost(flops, nbytes):
    return pl.CostEstimate(flops=int(flops), bytes_accessed=int(nbytes), transcendentals=0)


def hi_lo(state):
    high = state.astype(BF16)
    low = (state - high.astype(F32)).astype(BF16)
    return jnp.concatenate([high, low], axis=0)


def local_block(att_ref, rows, q_ref, k_ref, v_ref, pre, at):
    lower = lax.broadcasted_iota(jnp.int32, (BLK, BLK), 0) >= lax.broadcasted_iota(
        jnp.int32, (BLK, BLK), 1
    )
    for h in range(q_ref.shape[1] // DH):
        cols = slice(h * DH, (h + 1) * DH)
        q = q_ref[rows, cols]
        scores = lax.dot_general(
            q, k_ref[rows, cols], (((1,), (1,)), ((), ())), preferred_element_type=F32
        )
        scores = jnp.where(lower, scores, 0.0).astype(BF16)
        att_ref[rows, cols] = dot(scores, v_ref[rows, cols]) + dot(
            jnp.concatenate([q, q], axis=1), pre[at, h]
        )


def qkv_kernel(
    x_hbm, w_hbm, q_hbm, k_hbm, v_hbm, pre_hbm, tot_ref, att_hbm,
    x, w, q, k, v, pre, att, x_sem, w_sem, out_sem,
):
    steps = x_sem.shape[0] // 2
    tile = x.shape[0] // steps
    width = x.shape[1]
    half = width // 2
    heads = tot_ref.shape[0]
    blocks = tile // BLK
    inside = att.shape[0] // tile

    def tokens(i, part):
        at = (pl.ds(i * tile, tile), pl.ds(part * half, half))
        return pltpu.make_async_copy(x_hbm.at[at], x.at[at], x_sem.at[2 * i + part])

    def weight(which, part):
        at = pl.ds(part * half, half)
        return pltpu.make_async_copy(
            w_hbm.at[which, at], w.at[which, at], w_sem.at[2 * which + part]
        )

    for part in range(2):
        tokens(0, part).start()
        weight(1, part).start()
    for which in (2, 0):
        for part in range(2):
            weight(which, part).start()
    for i in range(1, steps):
        for part in range(2):
            tokens(i, part).start()

    pending = []

    def put(i, source, target, which):
        copy = pltpu.make_async_copy(source, target, out_sem.at[i, which])
        copy.start()
        pending.append(copy)

    state = [jnp.zeros((DH, DH), F32)] * heads
    for i in range(steps):
        rows = pl.ds(i * tile, tile)
        if i == 0:
            total = None
            for part in range(2):
                tokens(0, part).wait()
                weight(1, part).wait()
                cut = pl.ds(part * half, half)
                product = dot(x[rows, cut], w[1, cut])
                total = product if total is None else total + product
            k[rows] = total.astype(BF16)
        else:
            for part in range(2):
                tokens(i, part).wait()
            k[rows] = dot(x[rows], w[1]).astype(BF16)
        for which, out in ((2, v), (0, q)):
            if i == 0:
                for part in range(2):
                    weight(which, part).wait()
            out[rows] = dot(x[rows], w[which]).astype(BF16)
        for b in range(i * blocks, (i + 1) * blocks):
            block = slice(b * BLK, (b + 1) * BLK)
            for h in range(heads):
                cols = slice(h * DH, (h + 1) * DH)
                pre[b, h] = hi_lo(state[h])
                state[h] = state[h] + lax.dot_general(
                    k[block, cols], v[block, cols], (((0,), (0,)), ((), ())),
                    preferred_element_type=F32,
                )
            if i < inside:
                local_block(att, block, q, k, v, pre, b)
        put(i, q.at[rows], q_hbm.at[rows], 0)
        put(i, k.at[rows], k_hbm.at[rows], 1)
        put(i, v.at[rows], v_hbm.at[rows], 2)
        at = pl.ds(i * blocks, blocks)
        put(i, pre.at[at], pre_hbm.at[at], 3)
        if i < inside:
            put(i, att.at[rows], att_hbm.at[rows], 4)
    for h in range(heads):
        tot_ref[h] = state[h].astype(BF16)
    for copy in pending:
        copy.wait()


def project(x, w_qkv, inside, tile=512):
    tokens, width = x.shape
    feats = w_qkv.shape[2]
    heads = feats // DH
    steps = tokens // tile
    wide = (tokens, feats)
    states = (tokens // BLK, heads, 2 * DH, DH)
    anywhere = pl.BlockSpec(memory_space=pl.ANY)
    return pl.pallas_call(
        qkv_kernel,
        in_specs=[anywhere] * 2,
        out_specs=[anywhere] * 4 + [pl.BlockSpec(memory_space=pltpu.VMEM), anywhere],
        out_shape=[jax.ShapeDtypeStruct(wide, BF16)] * 3
        + [
            jax.ShapeDtypeStruct(states, BF16),
            jax.ShapeDtypeStruct((heads, DH, DH), BF16),
            jax.ShapeDtypeStruct(wide, F32),
        ],
        scratch_shapes=[
            pltpu.VMEM((tokens, width), BF16),
            pltpu.VMEM((3, width, feats), BF16),
            pltpu.VMEM(wide, BF16),
            pltpu.VMEM(wide, BF16),
            pltpu.VMEM(wide, BF16),
            pltpu.VMEM(states, BF16),
            pltpu.VMEM((inside * tile, feats), F32),
            pltpu.SemaphoreType.DMA((2 * steps,)),
            pltpu.SemaphoreType.DMA((6,)),
            pltpu.SemaphoreType.DMA((steps, 5)),
        ],
        cost_estimate=cost(6 * tokens * width * feats, 2 * tokens * width + 6 * width * feats),
        name="project",
    )(x, w_qkv)


def local_kernel(q_ref, k_ref, v_ref, pre_ref, att_in, att_ref):
    for b in range(q_ref.shape[0] // BLK):
        local_block(att_ref, slice(b * BLK, (b + 1) * BLK), q_ref, k_ref, v_ref, pre_ref, b)


def local_part(q, k, v, pre, att, piece, pieces, tile=256):
    tokens, feats = q.shape
    heads = feats // DH
    blocks = tile // BLK
    count = tokens // pieces
    start = piece * count // tile
    row = pl.BlockSpec((tile, feats), lambda i: (i + start, 0))
    return pl.pallas_call(
        local_kernel,
        grid=(count // tile,),
        in_specs=[
            row, row, row,
            pl.BlockSpec((blocks, heads, 2 * DH, DH), lambda i: (i + start, 0, 0, 0)),
            pl.BlockSpec(memory_space=pl.ANY),
        ],
        out_specs=row,
        out_shape=jax.ShapeDtypeStruct((tokens, feats), F32),
        input_output_aliases={4: 0},
        cost_estimate=cost(8 * count * feats * BLK, 14 * count * feats),
        name="local_part",
    )(q, k, v, pre, att)


def norm_rows(q_ref, att_ref, pair, gain_ref, n_ref, h):
    cols = slice(h * DH, (h + 1) * DH)
    q = q_ref[:, cols]
    att = att_ref[:, cols] + dot(jnp.concatenate([q, q], axis=1), pair)
    mean_sq = jnp.mean(att * att, axis=-1, keepdims=True)
    n_ref[:, cols] = (att * lax.rsqrt(mean_sq + 1e-06) * gain_ref[:, cols]).astype(BF16)


def start_kernel(
    head, core, y, x, q_ref, att_ref, core_ref, y1_ref, y2_ref, x1_ref, x2_ref, gain_ref,
    n_ref, pair_ref,
):
    takes = (
        (core[0] == 1, core_ref),
        (lax.rem(y[0], 2) == 1, y1_ref),
        (y[0] >= 2, y2_ref),
        (lax.rem(x[0], 2) == 1, x1_ref),
        (x[0] >= 2, x2_ref),
    )
    for h in range(core_ref.shape[0]):

        @pl.when(pl.program_id(0) == 0)
        def _():
            carried = jnp.zeros((DH, DH), F32)
            for take, ref in takes:
                carried = carried + jnp.where(take, ref[h].astype(F32), 0.0)
            pair_ref[h] = hi_lo(carried)

    for h in range(core_ref.shape[0]):
        norm_rows(q_ref, att_ref, pair_ref[h], gain_ref, n_ref, h)


def finish_kernel(head, core, y, x, q_ref, att_ref, pair_ref, gain_ref, n_ref):
    for h in range(pair_ref.shape[0]):
        norm_rows(q_ref, att_ref, pair_ref[h], gain_ref, n_ref, h)


def finish(place, direction, shift, q, att, received, gain, parts, tile=256):
    tokens, feats = q.shape
    count = tokens // parts
    per = count // tile
    heads = feats // DH

    def row(i, head, core, y, x):
        to = head[0] + direction * (1 - 2 * core[0]) + shift + parts
        return (lax.rem(to, parts) * per + i, 0)

    first = len(received) > 1
    normed = jax.ShapeDtypeStruct((count, feats), BF16)
    rows = pl.BlockSpec((tile, feats), lambda i, *place: (i, 0))
    whole = lambda a: pl.BlockSpec(a.shape, lambda i, *place: (0,) * len(a.shape))
    pair = jax.ShapeDtypeStruct((heads, 2 * DH, DH), BF16)
    return pl.pallas_call(
        start_kernel if first else finish_kernel,
        grid_spec=pltpu.PrefetchScalarGridSpec(
            num_scalar_prefetch=4,
            grid=(per,),
            in_specs=[pl.BlockSpec((tile, feats), row), pl.BlockSpec((tile, feats), row)]
            + [whole(a) for a in received]
            + [whole(gain)],
            out_specs=[rows, whole(pair)] if first else rows,
        ),
        out_shape=[normed, pair] if first else normed,
        cost_estimate=cost(2 * count * feats * DH * 2, count * feats * 8),
        name="finish",
    )(*place, q, att, *received, gain)


def first_kernel(
    n0_hbm, na_hbm, w0_hbm, wa_hbm, wb_hbm, mine_hbm, other_hbm,
    acc_out, wb_out, mine_out, other_out,
    n0, na, w0, wa, acc, n_sem, w_sem, out_sem, pass_sem,
):
    tiles = w_sem.shape[0]
    tile = acc.shape[1] // tiles
    columns = [slice(j * tile, (j + 1) * tile) for j in range(tiles)]
    rows = [
        pltpu.make_async_copy(n0_hbm, n0, n_sem.at[0]),
        pltpu.make_async_copy(na_hbm, na, n_sem.at[1]),
    ]
    weights = [
        [
            pltpu.make_async_copy(w0_hbm.at[:, cut], w0.at[:, cut], w_sem.at[j, 0]),
            pltpu.make_async_copy(wa_hbm.at[:, cut], wa.at[:, cut], w_sem.at[j, 1]),
        ]
        for j, cut in enumerate(columns)
    ]
    for which in range(2):
        rows[which].start()
        weights[0][which].start()
    for copies in weights[1:]:
        for copy in copies:
            copy.start()
    passed = [
        pltpu.make_async_copy(source, target, pass_sem.at[i])
        for i, (source, target) in enumerate(
            ((wb_hbm, wb_out), (mine_hbm, mine_out), (other_hbm, other_out))
        )
    ]
    for copy in passed:
        copy.start()
    for j, cut in enumerate(columns):
        if j == 0:
            rows[0].wait()
        weights[j][0].wait()
        total = dot(n0[...], w0[:, cut])
        if j == 0:
            rows[1].wait()
        weights[j][1].wait()
        acc[:, cut] = total + dot(na[...], wa[:, cut])
        copy = pltpu.make_async_copy(acc.at[:, cut], acc_out.at[:, cut], out_sem.at[j])
        copy.start()
        passed.append(copy)
    for copy in passed:
        copy.wait()


def last_kernel(
    core, acc_hbm, nb_hbm, nf_hbm, wb_hbm, mine_hbm, other_hbm, out_hbm,
    acc, nb, nf, wb, mine, other, out, n_sem, w_sem, out_sem,
):
    tiles = w_sem.shape[0]
    tile = out.shape[1] // tiles
    half = mine.shape[0]
    rows = [pltpu.make_async_copy(nb_hbm, nb, n_sem.at[0]), pltpu.make_async_copy(nf_hbm, nf, n_sem.at[1])]
    columns = [slice(j * tile, (j + 1) * tile) for j in range(tiles)]
    weights = [
        [
            pltpu.make_async_copy(source.at[:, cut], target.at[:, cut], w_sem.at[j, which])
            for which, (source, target) in enumerate(
                ((wb_hbm, wb), (mine_hbm, mine), (other_hbm, other), (acc_hbm, acc))
            )
        ]
        for j, cut in enumerate(columns)
    ]
    for which in range(2):
        rows[which].start()
        for copy in weights[0][which :: 2]:
            copy.start()
    for copies in weights[1:]:
        for copy in copies:
            copy.start()
    own = pl.multiple_of(core[0] * half, half)
    partner = pl.multiple_of((1 - core[0]) * half, half)
    pending = []
    for j, cut in enumerate(columns):
        if j == 0:
            rows[0].wait()
        weights[j][0].wait()
        total = dot(nb[...], wb[:, cut])
        if j == 0:
            rows[1].wait()
        weights[j][1].wait()
        total += dot(nf[:, pl.ds(own, half)], mine[:, cut])
        weights[j][2].wait()
        total += dot(nf[:, pl.ds(partner, half)], other[:, cut])
        weights[j][3].wait()
        out[:, cut] = (total + acc[:, cut]).astype(BF16)
        copy = pltpu.make_async_copy(out.at[:, cut], out_hbm.at[:, cut], out_sem.at[j])
        copy.start()
        pending.append(copy)
    for copy in pending:
        copy.wait()


def mix_first(normed, weights, later, tiles=2):
    rows, feats = normed[0].shape
    width = weights[0].shape[1]
    operands = [*normed, *weights]
    return pl.pallas_call(
        first_kernel,
        in_specs=[pl.BlockSpec(memory_space=pltpu.HBM)] * (len(operands) + len(later)),
        out_specs=[pl.BlockSpec(memory_space=pl.ANY)] * (1 + len(later)),
        scratch_shapes=[pltpu.VMEM(a.shape, a.dtype) for a in operands]
        + [
            pltpu.VMEM((rows, width), F32),
            pltpu.SemaphoreType.DMA((2,)),
            pltpu.SemaphoreType.DMA((tiles, 2)),
            pltpu.SemaphoreType.DMA((tiles,)),
            pltpu.SemaphoreType.DMA((len(later),)),
        ],
        out_shape=[jax.ShapeDtypeStruct((rows, width), F32)]
        + [jax.ShapeDtypeStruct(a.shape, a.dtype) for a in later],
        cost_estimate=cost(4 * rows * feats * width, 8 * rows * width),
        compiler_params=pltpu.CompilerParams(vmem_limit_bytes=24 << 20),
        name="mix_first",
    )(*operands, *later)


def mix_last(core, acc, normed, weights, tiles=2):
    rows, feats = normed[0].shape
    width = acc.shape[1]
    anywhere = pl.BlockSpec(memory_space=pl.ANY)
    operands = [acc, *normed, *weights]
    return pl.pallas_call(
        last_kernel,
        grid_spec=pltpu.PrefetchScalarGridSpec(
            num_scalar_prefetch=1,
            grid=(1,),
            in_specs=[anywhere] * len(operands),
            out_specs=anywhere,
            scratch_shapes=[pltpu.VMEM(a.shape, a.dtype) for a in operands]
            + [
                pltpu.VMEM((rows, width), BF16),
                pltpu.SemaphoreType.DMA((2,)),
                pltpu.SemaphoreType.DMA((tiles, 4)),
                pltpu.SemaphoreType.DMA((tiles,)),
            ],
        ),
        out_shape=jax.ShapeDtypeStruct((rows, width), BF16),
        cost_estimate=cost(4 * rows * feats * width, 8 * rows * width),
        compiler_params=pltpu.CompilerParams(vmem_limit_bytes=24 << 20),
        name="mix_last",
    )(core, *operands)


def pair_up(size, stride, total, first):
    pairs = []
    for i in range(total):
        at = (i // stride) % size
        to = at ^ 1 if first else (at + (1 if at % 2 else -1)) % size
        pairs.append((i, i + (to - at) * stride))
    return pairs


def pair_rounds(value, stride, total):
    value = value.astype(BF16)
    other = lax.ppermute(value, "seq", pair_up(4, stride, total, True))
    pair = (value.astype(F32) + other.astype(F32)).astype(BF16)
    far = lax.ppermute(pair, "seq", pair_up(4, stride, total, False))
    return other, far, pair.astype(F32) + far.astype(F32)


def layer(inputs, w_qkv, norm_gain, w_out):
    parts = lax.axis_size("head")
    total = lax.axis_size("seq")
    seq = lax.axis_index("seq")
    core = lax.rem(seq, 2)
    y = lax.rem(seq // 2, 4)
    x = seq // 8
    head = lax.axis_index("head")
    core_id = core.astype(jnp.int32).reshape(1)
    place = [a.astype(jnp.int32).reshape(1) for a in (head, core, y, x)]

    def along(direction):
        pairs = []
        for i in range(total):
            shift = direction * (1 - 2 * (i % 2))
            for h in range(parts):
                pairs.append((i * parts + h, i * parts + (h + shift) % parts))
        return pairs

    partner = [(i, i ^ 1) for i in range(total)]

    def swap(a):
        return lax.ppermute(a, "seq", partner)

    def send(a, direction):
        return lax.ppermute(a, ("seq", "head"), along(direction))

    near = send(w_out, 1)
    rows = w_out.shape[0] // 2
    far = lax.dynamic_slice_in_dim(near, core * rows, rows, 0)
    far = send(far, 1)
    near_other = swap(near)
    far_other = swap(far)

    q, k, v, pre, tot, att = project(inputs, w_qkv, 1)
    other = swap(tot)
    for piece in range(1, 4):
        att = local_part(q, k, v, pre, att, piece, 4)
    y1, y2, row = pair_rounds(tot.astype(F32) + other.astype(F32), 2, total)
    x1, x2, _ = pair_rounds(row, 8, total)
    received = (other, y1, y2, x1, x2)

    gain = norm_gain.reshape(1, -1)
    nf, pair = finish(place, 0, 2, q, att, received, gain, parts)
    nf = send(nf, 1)
    na = send(finish(place, 1, 0, q, att, (pair,), gain, parts), 1)
    nb = send(finish(place, -1, 0, q, att, (pair,), gain, parts), -1)
    nf = send(nf, 1)
    n0 = finish(place, 0, 0, q, att, (pair,), gain, parts)
    later = [near_other, far, far_other]
    acc, *later = mix_first([n0, na], [w_out, near], later)
    return mix_last(core_id, acc, [nb, nf], later)


def solution(mesh):
    return jax.shard_map(
        layer,
        mesh=mesh,
        in_specs=(P("seq", None), P(None, None, "head"), P("head"), P("head", None)),
        out_specs=P(("seq", "head"), None),
        check_vma=False,
    )
```

```python
import jax
import jax.numpy as jnp
from jax import lax
from jax.experimental import pallas as pl
from jax.experimental.pallas import tpu as pltpu
from jax.sharding import PartitionSpec as P


DH = 128
BLK = 256
F32 = jnp.float32
BF16 = jnp.bfloat16


def dot(a, b):
    return jnp.dot(a, b, preferred_element_type=F32)


def cost(flops, nbytes):
    return pl.CostEstimate(flops=int(flops), bytes_accessed=int(nbytes), transcendentals=0)


def hi_lo(state):
    high = state.astype(BF16)
    low = (state - high.astype(F32)).astype(BF16)
    return jnp.concatenate([high, low], axis=0)


def local_block(att_ref, rows, q_ref, k_ref, v_ref, pre, at):
    lower = lax.broadcasted_iota(jnp.int32, (BLK, BLK), 0) >= lax.broadcasted_iota(
        jnp.int32, (BLK, BLK), 1
    )
    for h in range(q_ref.shape[1] // DH):
        cols = slice(h * DH, (h + 1) * DH)
        q = q_ref[rows, cols]
        scores = lax.dot_general(
            q, k_ref[rows, cols], (((1,), (1,)), ((), ())), preferred_element_type=F32
        )
        scores = jnp.where(lower, scores, 0.0).astype(BF16)
        att_ref[rows, cols] = dot(scores, v_ref[rows, cols]) + dot(
            jnp.concatenate([q, q], axis=1), pre[at, h]
        )


def qkv_kernel(
    x_hbm, w_hbm, q_hbm, k_hbm, v_hbm, pre_hbm, tot_ref, att_hbm,
    x, w, q, k, v, pre, att, x_sem, w_sem, out_sem,
):
    steps = x_sem.shape[0] // 2
    tile = x.shape[0] // steps
    width = x.shape[1]
    half = width // 2
    heads = tot_ref.shape[0]
    blocks = tile // BLK
    inside = att.shape[0] // tile

    def tokens(i, part):
        at = (pl.ds(i * tile, tile), pl.ds(part * half, half))
        return pltpu.make_async_copy(x_hbm.at[at], x.at[at], x_sem.at[2 * i + part])

    def weight(which, part):
        at = pl.ds(part * half, half)
        return pltpu.make_async_copy(
            w_hbm.at[which, at], w.at[which, at], w_sem.at[2 * which + part]
        )

    for part in range(2):
        tokens(0, part).start()
        weight(1, part).start()
    for which in (2, 0):
        for part in range(2):
            weight(which, part).start()
    for i in range(1, steps):
        for part in range(2):
            tokens(i, part).start()

    pending = []

    def put(i, source, target, which):
        copy = pltpu.make_async_copy(source, target, out_sem.at[i, which])
        copy.start()
        pending.append(copy)

    state = [jnp.zeros((DH, DH), F32)] * heads
    for i in range(steps):
        rows = pl.ds(i * tile, tile)
        if i == 0:
            total = None
            for part in range(2):
                tokens(0, part).wait()
                weight(1, part).wait()
                cut = pl.ds(part * half, half)
                product = dot(x[rows, cut], w[1, cut])
                total = product if total is None else total + product
            k[rows] = total.astype(BF16)
        else:
            for part in range(2):
                tokens(i, part).wait()
            k[rows] = dot(x[rows], w[1]).astype(BF16)
        for which, out in ((2, v), (0, q)):
            if i == 0:
                for part in range(2):
                    weight(which, part).wait()
            out[rows] = dot(x[rows], w[which]).astype(BF16)
        for b in range(i * blocks, (i + 1) * blocks):
            block = slice(b * BLK, (b + 1) * BLK)
            for h in range(heads):
                cols = slice(h * DH, (h + 1) * DH)
                pre[b, h] = hi_lo(state[h])
                state[h] = state[h] + lax.dot_general(
                    k[block, cols], v[block, cols], (((0,), (0,)), ((), ())),
                    preferred_element_type=F32,
                )
            if i < inside:
                local_block(att, block, q, k, v, pre, b)
        put(i, q.at[rows], q_hbm.at[rows], 0)
        put(i, k.at[rows], k_hbm.at[rows], 1)
        put(i, v.at[rows], v_hbm.at[rows], 2)
        at = pl.ds(i * blocks, blocks)
        put(i, pre.at[at], pre_hbm.at[at], 3)
        if i < inside:
            put(i, att.at[rows], att_hbm.at[rows], 4)
    for h in range(heads):
        tot_ref[h] = state[h].astype(BF16)
    for copy in pending:
        copy.wait()


def project(x, w_qkv, inside, tile=512):
    tokens, width = x.shape
    feats = w_qkv.shape[2]
    heads = feats // DH
    steps = tokens // tile
    wide = (tokens, feats)
    states = (tokens // BLK, heads, 2 * DH, DH)
    anywhere = pl.BlockSpec(memory_space=pl.ANY)
    return pl.pallas_call(
        qkv_kernel,
        in_specs=[anywhere] * 2,
        out_specs=[anywhere] * 4 + [pl.BlockSpec(memory_space=pltpu.VMEM), anywhere],
        out_shape=[jax.ShapeDtypeStruct(wide, BF16)] * 3
        + [
            jax.ShapeDtypeStruct(states, BF16),
            jax.ShapeDtypeStruct((heads, DH, DH), BF16),
            jax.ShapeDtypeStruct(wide, F32),
        ],
        scratch_shapes=[
            pltpu.VMEM((tokens, width), BF16),
            pltpu.VMEM((3, width, feats), BF16),
            pltpu.VMEM(wide, BF16),
            pltpu.VMEM(wide, BF16),
            pltpu.VMEM(wide, BF16),
            pltpu.VMEM(states, BF16),
            pltpu.VMEM((inside * tile, feats), F32),
            pltpu.SemaphoreType.DMA((2 * steps,)),
            pltpu.SemaphoreType.DMA((6,)),
            pltpu.SemaphoreType.DMA((steps, 5)),
        ],
        cost_estimate=cost(6 * tokens * width * feats, 2 * tokens * width + 6 * width * feats),
        name="project",
    )(x, w_qkv)


def local_kernel(q_ref, k_ref, v_ref, pre_ref, att_in, att_ref):
    for b in range(q_ref.shape[0] // BLK):
        local_block(att_ref, slice(b * BLK, (b + 1) * BLK), q_ref, k_ref, v_ref, pre_ref, b)


def local_part(q, k, v, pre, att, piece, pieces, tile=256):
    tokens, feats = q.shape
    heads = feats // DH
    blocks = tile // BLK
    count = tokens // pieces
    start = piece * count // tile
    row = pl.BlockSpec((tile, feats), lambda i: (i + start, 0))
    return pl.pallas_call(
        local_kernel,
        grid=(count // tile,),
        in_specs=[
            row, row, row,
            pl.BlockSpec((blocks, heads, 2 * DH, DH), lambda i: (i + start, 0, 0, 0)),
            pl.BlockSpec(memory_space=pl.ANY),
        ],
        out_specs=row,
        out_shape=jax.ShapeDtypeStruct((tokens, feats), F32),
        input_output_aliases={4: 0},
        cost_estimate=cost(8 * count * feats * BLK, 14 * count * feats),
        name="local_part",
    )(q, k, v, pre, att)


def norm_rows(q_ref, att_ref, pair, gain_ref, n_ref, h):
    cols = slice(h * DH, (h + 1) * DH)
    q = q_ref[:, cols]
    att = att_ref[:, cols] + dot(jnp.concatenate([q, q], axis=1), pair)
    mean_sq = jnp.mean(att * att, axis=-1, keepdims=True)
    n_ref[:, cols] = (att * lax.rsqrt(mean_sq + 1e-06) * gain_ref[:, cols]).astype(BF16)


def start_kernel(
    head, core, y, x, q_ref, att_ref, core_ref, y1_ref, y2_ref, x1_ref, x2_ref, gain_ref,
    n_ref, pair_ref,
):
    takes = (
        (core[0] == 1, core_ref),
        (lax.rem(y[0], 2) == 1, y1_ref),
        (y[0] >= 2, y2_ref),
        (lax.rem(x[0], 2) == 1, x1_ref),
        (x[0] >= 2, x2_ref),
    )
    for h in range(core_ref.shape[0]):

        @pl.when(pl.program_id(0) == 0)
        def _():
            carried = jnp.zeros((DH, DH), F32)
            for take, ref in takes:
                carried = carried + jnp.where(take, ref[h].astype(F32), 0.0)
            pair_ref[h] = hi_lo(carried)

    for h in range(core_ref.shape[0]):
        norm_rows(q_ref, att_ref, pair_ref[h], gain_ref, n_ref, h)


def finish_kernel(head, core, y, x, q_ref, att_ref, pair_ref, gain_ref, n_ref):
    for h in range(pair_ref.shape[0]):
        norm_rows(q_ref, att_ref, pair_ref[h], gain_ref, n_ref, h)


def finish(place, direction, shift, q, att, received, gain, parts, tile=256):
    tokens, feats = q.shape
    count = tokens // parts
    per = count // tile
    heads = feats // DH

    def row(i, head, core, y, x):
        to = head[0] + direction * (1 - 2 * core[0]) + shift + parts
        return (lax.rem(to, parts) * per + i, 0)

    first = len(received) > 1
    normed = jax.ShapeDtypeStruct((count, feats), BF16)
    rows = pl.BlockSpec((tile, feats), lambda i, *place: (i, 0))
    whole = lambda a: pl.BlockSpec(a.shape, lambda i, *place: (0,) * len(a.shape))
    pair = jax.ShapeDtypeStruct((heads, 2 * DH, DH), BF16)
    return pl.pallas_call(
        start_kernel if first else finish_kernel,
        grid_spec=pltpu.PrefetchScalarGridSpec(
            num_scalar_prefetch=4,
            grid=(per,),
            in_specs=[pl.BlockSpec((tile, feats), row), pl.BlockSpec((tile, feats), row)]
            + [whole(a) for a in received]
            + [whole(gain)],
            out_specs=[rows, whole(pair)] if first else rows,
        ),
        out_shape=[normed, pair] if first else normed,
        cost_estimate=cost(2 * count * feats * DH * 2, count * feats * 8),
        name="finish",
    )(*place, q, att, *received, gain)


def own_kernel(n_ref, w_ref, *rest):
    later, (acc_ref, *passed, sem) = rest[: len(rest) // 2 - 1], rest[len(rest) // 2 - 1 :]
    copies = [
        pltpu.make_async_copy(source, target, sem.at[i])
        for i, (source, target) in enumerate(zip(later, passed))
    ]

    @pl.when(pl.program_id(0) == 0)
    def _():
        for copy in copies:
            copy.start()

    acc_ref[...] = dot(n_ref[...], w_ref[...])

    @pl.when(pl.program_id(0) == pl.num_programs(0) - 1)
    def _():
        for copy in copies:
            copy.wait()


def mix_own(normed, weight, later, tile=512):
    rows, feats = normed.shape
    width = weight.shape[1]
    anywhere = [pl.BlockSpec(memory_space=pl.ANY)] * len(later)
    return pl.pallas_call(
        own_kernel,
        grid=(width // tile,),
        in_specs=[
            pl.BlockSpec((rows, feats), lambda i: (0, 0)),
            pl.BlockSpec((feats, tile), lambda i: (0, i)),
        ]
        + anywhere,
        out_specs=[pl.BlockSpec((rows, tile), lambda i: (0, i))] + anywhere,
        out_shape=[jax.ShapeDtypeStruct((rows, width), F32)]
        + [jax.ShapeDtypeStruct(a.shape, a.dtype) for a in later],
        scratch_shapes=[pltpu.SemaphoreType.DMA((len(later),))],
        cost_estimate=cost(2 * rows * feats * width, 8 * rows * width),
        compiler_params=pltpu.CompilerParams(vmem_limit_bytes=24 << 20),
        name="mix_own",
    )(normed, weight, *later)


def last_kernel(core, acc_ref, na, nb, nf, wa, wb, mine_ref, other_ref, out_ref):
    half = mine_ref.shape[0]
    mine = pl.multiple_of(core[0] * half, half)
    other = pl.multiple_of((1 - core[0]) * half, half)
    acc = dot(na[...], wa[...]) + dot(nb[...], wb[...])
    acc += dot(nf[:, pl.ds(mine, half)], mine_ref[...])
    acc += dot(nf[:, pl.ds(other, half)], other_ref[...])
    out_ref[...] = (acc + acc_ref[...]).astype(BF16)


def mix_last(core, acc, normed, weights, tile=512):
    rows, feats = normed[0].shape
    width = acc.shape[1]
    column = lambda a: pl.BlockSpec((a.shape[0], tile), lambda i, core: (0, i))
    return pl.pallas_call(
        last_kernel,
        grid_spec=pltpu.PrefetchScalarGridSpec(
            num_scalar_prefetch=1,
            grid=(width // tile,),
            in_specs=[column(acc)]
            + [pl.BlockSpec(a.shape, lambda i, core: (0, 0)) for a in normed]
            + [column(a) for a in weights],
            out_specs=pl.BlockSpec((rows, tile), lambda i, core: (0, i)),
        ),
        out_shape=jax.ShapeDtypeStruct((rows, width), BF16),
        cost_estimate=cost(6 * rows * feats * width, 8 * rows * width),
        compiler_params=pltpu.CompilerParams(vmem_limit_bytes=24 << 20),
        name="mix_last",
    )(core, acc, *normed, *weights)


def pair_up(size, stride, total, first):
    pairs = []
    for i in range(total):
        at = (i // stride) % size
        to = at ^ 1 if first else (at + (1 if at % 2 else -1)) % size
        pairs.append((i, i + (to - at) * stride))
    return pairs


def pair_rounds(value, stride, total):
    value = value.astype(BF16)
    other = lax.ppermute(value, "seq", pair_up(4, stride, total, True))
    pair = (value.astype(F32) + other.astype(F32)).astype(BF16)
    far = lax.ppermute(pair, "seq", pair_up(4, stride, total, False))
    return other, far, pair.astype(F32) + far.astype(F32)


def layer(inputs, w_qkv, norm_gain, w_out):
    parts = lax.axis_size("head")
    total = lax.axis_size("seq")
    seq = lax.axis_index("seq")
    core = lax.rem(seq, 2)
    y = lax.rem(seq // 2, 4)
    x = seq // 8
    head = lax.axis_index("head")
    core_id = core.astype(jnp.int32).reshape(1)
    place = [a.astype(jnp.int32).reshape(1) for a in (head, core, y, x)]

    def along(direction):
        pairs = []
        for i in range(total):
            shift = direction * (1 - 2 * (i % 2))
            for h in range(parts):
                pairs.append((i * parts + h, i * parts + (h + shift) % parts))
        return pairs

    partner = [(i, i ^ 1) for i in range(total)]

    def swap(a):
        return lax.ppermute(a, "seq", partner)

    def send(a, direction):
        return lax.ppermute(a, ("seq", "head"), along(direction))

    near = send(w_out, 1)
    rows = w_out.shape[0] // 2
    far = lax.dynamic_slice_in_dim(near, core * rows, rows, 0)
    far = send(far, 1)
    near_other = swap(near)
    far_other = swap(far)

    q, k, v, pre, tot, att = project(inputs, w_qkv, 1)
    other = swap(tot)
    for piece in range(1, 4):
        att = local_part(q, k, v, pre, att, piece, 4)
    y1, y2, row = pair_rounds(tot.astype(F32) + other.astype(F32), 2, total)
    x1, x2, _ = pair_rounds(row, 8, total)
    received = (other, y1, y2, x1, x2)

    gain = norm_gain.reshape(1, -1)
    nf, pair = finish(place, 0, 2, q, att, received, gain, parts)
    nf = send(nf, 1)
    na = send(finish(place, 1, 0, q, att, (pair,), gain, parts), 1)
    nb = send(finish(place, -1, 0, q, att, (pair,), gain, parts), -1)
    nf = send(nf, 1)
    n0 = finish(place, 0, 0, q, att, (pair,), gain, parts)
    acc, *weights = mix_own(n0, w_out, [near, near_other, far, far_other])
    return mix_last(core_id, acc, [na, nb, nf], weights)


def solution(mesh):
    return jax.shard_map(
        layer,
        mesh=mesh,
        in_specs=(P("seq", None), P(None, None, "head"), P("head"), P("head", None)),
        out_specs=P(("seq", "head"), None),
        check_vma=False,
    )
```

```python
import jax
import jax.numpy as jnp
from jax import lax
from jax.experimental import pallas as pl
from jax.experimental.pallas import tpu as pltpu
from jax.sharding import PartitionSpec as P


DH = 128
BLK = 256
F32 = jnp.float32
BF16 = jnp.bfloat16


def dot(a, b):
    return jnp.dot(a, b, preferred_element_type=F32)


def cost(flops, nbytes):
    return pl.CostEstimate(flops=int(flops), bytes_accessed=int(nbytes), transcendentals=0)


def hi_lo(state):
    high = state.astype(BF16)
    low = (state - high.astype(F32)).astype(BF16)
    return jnp.concatenate([high, low], axis=0)


def local_block(att_ref, rows, q_ref, k_ref, v_ref, pre, at):
    lower = lax.broadcasted_iota(jnp.int32, (BLK, BLK), 0) >= lax.broadcasted_iota(
        jnp.int32, (BLK, BLK), 1
    )
    for h in range(q_ref.shape[1] // DH):
        cols = slice(h * DH, (h + 1) * DH)
        q = q_ref[rows, cols]
        scores = lax.dot_general(
            q, k_ref[rows, cols], (((1,), (1,)), ((), ())), preferred_element_type=F32
        )
        scores = jnp.where(lower, scores, 0.0).astype(BF16)
        att_ref[rows, cols] = dot(scores, v_ref[rows, cols]) + dot(
            jnp.concatenate([q, q], axis=1), pre[at, h]
        )


def qkv_kernel(
    x_hbm, w_hbm, q_hbm, k_hbm, v_hbm, pre_hbm, tot_ref, att_hbm,
    x, w, q, k, v, pre, att, x_sem, w_sem, out_sem,
):
    steps = x_sem.shape[0] // 2
    tile = x.shape[0] // steps
    width = x.shape[1]
    half = width // 2
    heads = tot_ref.shape[0]
    blocks = tile // BLK
    inside = att.shape[0] // tile

    def tokens(i, part):
        at = (pl.ds(i * tile, tile), pl.ds(part * half, half))
        return pltpu.make_async_copy(x_hbm.at[at], x.at[at], x_sem.at[2 * i + part])

    def weight(which, part):
        at = pl.ds(part * half, half)
        return pltpu.make_async_copy(
            w_hbm.at[which, at], w.at[which, at], w_sem.at[2 * which + part]
        )

    for part in range(2):
        tokens(0, part).start()
        weight(1, part).start()
    for which in (2, 0):
        for part in range(2):
            weight(which, part).start()
    for i in range(1, steps):
        for part in range(2):
            tokens(i, part).start()

    pending = []

    def put(i, source, target, which):
        copy = pltpu.make_async_copy(source, target, out_sem.at[i, which])
        copy.start()
        pending.append(copy)

    state = [jnp.zeros((DH, DH), F32)] * heads
    for i in range(steps):
        rows = pl.ds(i * tile, tile)
        if i == 0:
            total = None
            for part in range(2):
                tokens(0, part).wait()
                weight(1, part).wait()
                cut = pl.ds(part * half, half)
                product = dot(x[rows, cut], w[1, cut])
                total = product if total is None else total + product
            k[rows] = total.astype(BF16)
        else:
            for part in range(2):
                tokens(i, part).wait()
            k[rows] = dot(x[rows], w[1]).astype(BF16)
        for which, out in ((2, v), (0, q)):
            if i == 0:
                for part in range(2):
                    weight(which, part).wait()
            out[rows] = dot(x[rows], w[which]).astype(BF16)
        for b in range(i * blocks, (i + 1) * blocks):
            block = slice(b * BLK, (b + 1) * BLK)
            for h in range(heads):
                cols = slice(h * DH, (h + 1) * DH)
                pre[b, h] = hi_lo(state[h])
                state[h] = state[h] + lax.dot_general(
                    k[block, cols], v[block, cols], (((0,), (0,)), ((), ())),
                    preferred_element_type=F32,
                )
            if i < inside:
                local_block(att, block, q, k, v, pre, b)
        put(i, q.at[rows], q_hbm.at[rows], 0)
        put(i, k.at[rows], k_hbm.at[rows], 1)
        put(i, v.at[rows], v_hbm.at[rows], 2)
        at = pl.ds(i * blocks, blocks)
        put(i, pre.at[at], pre_hbm.at[at], 3)
        if i < inside:
            put(i, att.at[rows], att_hbm.at[rows], 4)
    for h in range(heads):
        tot_ref[h] = state[h].astype(BF16)
    for copy in pending:
        copy.wait()


def project(x, w_qkv, inside, tile=512):
    tokens, width = x.shape
    feats = w_qkv.shape[2]
    heads = feats // DH
    steps = tokens // tile
    wide = (tokens, feats)
    states = (tokens // BLK, heads, 2 * DH, DH)
    anywhere = pl.BlockSpec(memory_space=pl.ANY)
    return pl.pallas_call(
        qkv_kernel,
        in_specs=[anywhere] * 2,
        out_specs=[anywhere] * 4 + [pl.BlockSpec(memory_space=pltpu.VMEM), anywhere],
        out_shape=[jax.ShapeDtypeStruct(wide, BF16)] * 3
        + [
            jax.ShapeDtypeStruct(states, BF16),
            jax.ShapeDtypeStruct((heads, DH, DH), BF16),
            jax.ShapeDtypeStruct(wide, F32),
        ],
        scratch_shapes=[
            pltpu.VMEM((tokens, width), BF16),
            pltpu.VMEM((3, width, feats), BF16),
            pltpu.VMEM(wide, BF16),
            pltpu.VMEM(wide, BF16),
            pltpu.VMEM(wide, BF16),
            pltpu.VMEM(states, BF16),
            pltpu.VMEM((inside * tile, feats), F32),
            pltpu.SemaphoreType.DMA((2 * steps,)),
            pltpu.SemaphoreType.DMA((6,)),
            pltpu.SemaphoreType.DMA((steps, 5)),
        ],
        cost_estimate=cost(6 * tokens * width * feats, 2 * tokens * width + 6 * width * feats),
        name="project",
    )(x, w_qkv)


def local_kernel(q_ref, k_ref, v_ref, pre_ref, att_in, att_ref):
    for b in range(q_ref.shape[0] // BLK):
        local_block(att_ref, slice(b * BLK, (b + 1) * BLK), q_ref, k_ref, v_ref, pre_ref, b)


def local_part(q, k, v, pre, att, piece, pieces, tile=256):
    tokens, feats = q.shape
    heads = feats // DH
    blocks = tile // BLK
    count = tokens // pieces
    start = piece * count // tile
    row = pl.BlockSpec((tile, feats), lambda i: (i + start, 0))
    return pl.pallas_call(
        local_kernel,
        grid=(count // tile,),
        in_specs=[
            row, row, row,
            pl.BlockSpec((blocks, heads, 2 * DH, DH), lambda i: (i + start, 0, 0, 0)),
            pl.BlockSpec(memory_space=pl.ANY),
        ],
        out_specs=row,
        out_shape=jax.ShapeDtypeStruct((tokens, feats), F32),
        input_output_aliases={4: 0},
        cost_estimate=cost(8 * count * feats * BLK, 14 * count * feats),
        name="local_part",
    )(q, k, v, pre, att)


def norm_rows(q_ref, att_ref, pair, gain_ref, n_ref, h):
    cols = slice(h * DH, (h + 1) * DH)
    q = q_ref[:, cols]
    att = att_ref[:, cols] + dot(jnp.concatenate([q, q], axis=1), pair)
    mean_sq = jnp.mean(att * att, axis=-1, keepdims=True)
    n_ref[:, cols] = (att * lax.rsqrt(mean_sq + 1e-06) * gain_ref[:, cols]).astype(BF16)


def start_kernel(
    head, core, y, x, q_ref, att_ref, core_ref, y1_ref, y2_ref, x1_ref, x2_ref, gain_ref,
    n_ref, pair_ref,
):
    takes = (
        (core[0] == 1, core_ref),
        (lax.rem(y[0], 2) == 1, y1_ref),
        (y[0] >= 2, y2_ref),
        (lax.rem(x[0], 2) == 1, x1_ref),
        (x[0] >= 2, x2_ref),
    )
    for h in range(core_ref.shape[0]):

        @pl.when(pl.program_id(0) == 0)
        def _():
            carried = jnp.zeros((DH, DH), F32)
            for take, ref in takes:
                carried = carried + jnp.where(take, ref[h].astype(F32), 0.0)
            pair_ref[h] = hi_lo(carried)

    for h in range(core_ref.shape[0]):
        norm_rows(q_ref, att_ref, pair_ref[h], gain_ref, n_ref, h)


def finish_kernel(head, core, y, x, q_ref, att_ref, pair_ref, gain_ref, n_ref):
    for h in range(pair_ref.shape[0]):
        norm_rows(q_ref, att_ref, pair_ref[h], gain_ref, n_ref, h)


def finish(place, direction, shift, q, att, received, gain, parts, tile=256):
    tokens, feats = q.shape
    count = tokens // parts
    per = count // tile
    heads = feats // DH

    def row(i, head, core, y, x):
        to = head[0] + direction * (1 - 2 * core[0]) + shift + parts
        return (lax.rem(to, parts) * per + i, 0)

    first = len(received) > 1
    normed = jax.ShapeDtypeStruct((count, feats), BF16)
    rows = pl.BlockSpec((tile, feats), lambda i, *place: (i, 0))
    whole = lambda a: pl.BlockSpec(a.shape, lambda i, *place: (0,) * len(a.shape))
    pair = jax.ShapeDtypeStruct((heads, 2 * DH, DH), BF16)
    return pl.pallas_call(
        start_kernel if first else finish_kernel,
        grid_spec=pltpu.PrefetchScalarGridSpec(
            num_scalar_prefetch=4,
            grid=(per,),
            in_specs=[pl.BlockSpec((tile, feats), row), pl.BlockSpec((tile, feats), row)]
            + [whole(a) for a in received]
            + [whole(gain)],
            out_specs=[rows, whole(pair)] if first else rows,
        ),
        out_shape=[normed, pair] if first else normed,
        cost_estimate=cost(2 * count * feats * DH * 2, count * feats * 8),
        name="finish",
    )(*place, q, att, *received, gain)


def own_kernel(n_ref, w_ref, *rest):
    later, (acc_ref, *passed, sem) = rest[: len(rest) // 2 - 1], rest[len(rest) // 2 - 1 :]
    copies = [
        pltpu.make_async_copy(source, target, sem.at[i])
        for i, (source, target) in enumerate(zip(later, passed))
    ]

    @pl.when(pl.program_id(0) == 0)
    def _():
        for copy in copies:
            copy.start()

    acc_ref[...] = dot(n_ref[...], w_ref[...])

    @pl.when(pl.program_id(0) == pl.num_programs(0) - 1)
    def _():
        for copy in copies:
            copy.wait()


def mix_own(normed, weight, later, tile=512):
    rows, feats = normed.shape
    width = weight.shape[1]
    anywhere = [pl.BlockSpec(memory_space=pl.ANY)] * len(later)
    return pl.pallas_call(
        own_kernel,
        grid=(width // tile,),
        in_specs=[
            pl.BlockSpec((rows, feats), lambda i: (0, 0)),
            pl.BlockSpec((feats, tile), lambda i: (0, i)),
        ]
        + anywhere,
        out_specs=[pl.BlockSpec((rows, tile), lambda i: (0, i))] + anywhere,
        out_shape=[jax.ShapeDtypeStruct((rows, width), F32)]
        + [jax.ShapeDtypeStruct(a.shape, a.dtype) for a in later],
        scratch_shapes=[pltpu.SemaphoreType.DMA((len(later),))],
        cost_estimate=cost(2 * rows * feats * width, 8 * rows * width),
        compiler_params=pltpu.CompilerParams(vmem_limit_bytes=24 << 20),
        name="mix_own",
    )(normed, weight, *later)


def middle_kernel(acc_ref, n_ref, w_ref, out_ref):
    out_ref[...] = acc_ref[...] + dot(n_ref[...], w_ref[...])


def mix_middle(acc, normed, weight, tile=512):
    rows, feats = normed.shape
    width = acc.shape[1]
    column = lambda a: pl.BlockSpec((a.shape[0], tile), lambda i: (0, i))
    return pl.pallas_call(
        middle_kernel,
        grid=(width // tile,),
        in_specs=[column(acc), pl.BlockSpec((rows, feats), lambda i: (0, 0)), column(weight)],
        out_specs=column(acc),
        out_shape=jax.ShapeDtypeStruct((rows, width), F32),
        input_output_aliases={0: 0},
        cost_estimate=cost(2 * rows * feats * width, 8 * rows * width),
        compiler_params=pltpu.CompilerParams(vmem_limit_bytes=24 << 20),
        name="mix_middle",
    )(acc, normed, weight)


def last_kernel(core, acc_ref, nb, nf, wb, mine_ref, other_ref, out_ref):
    half = mine_ref.shape[0]
    mine = pl.multiple_of(core[0] * half, half)
    other = pl.multiple_of((1 - core[0]) * half, half)
    acc = dot(nb[...], wb[...])
    acc += dot(nf[:, pl.ds(mine, half)], mine_ref[...])
    acc += dot(nf[:, pl.ds(other, half)], other_ref[...])
    out_ref[...] = (acc + acc_ref[...]).astype(BF16)


def mix_last(core, acc, normed, weights, tile=512):
    rows, feats = normed[0].shape
    width = acc.shape[1]
    column = lambda a: pl.BlockSpec((a.shape[0], tile), lambda i, core: (0, i))
    return pl.pallas_call(
        last_kernel,
        grid_spec=pltpu.PrefetchScalarGridSpec(
            num_scalar_prefetch=1,
            grid=(width // tile,),
            in_specs=[column(acc)]
            + [pl.BlockSpec(a.shape, lambda i, core: (0, 0)) for a in normed]
            + [column(a) for a in weights],
            out_specs=pl.BlockSpec((rows, tile), lambda i, core: (0, i)),
        ),
        out_shape=jax.ShapeDtypeStruct((rows, width), BF16),
        cost_estimate=cost(4 * rows * feats * width, 8 * rows * width),
        compiler_params=pltpu.CompilerParams(vmem_limit_bytes=24 << 20),
        name="mix_last",
    )(core, acc, *normed, *weights)


def pair_up(size, stride, total, first):
    pairs = []
    for i in range(total):
        at = (i // stride) % size
        to = at ^ 1 if first else (at + (1 if at % 2 else -1)) % size
        pairs.append((i, i + (to - at) * stride))
    return pairs


def pair_rounds(value, stride, total):
    value = value.astype(BF16)
    other = lax.ppermute(value, "seq", pair_up(4, stride, total, True))
    pair = (value.astype(F32) + other.astype(F32)).astype(BF16)
    far = lax.ppermute(pair, "seq", pair_up(4, stride, total, False))
    return other, far, pair.astype(F32) + far.astype(F32)


def layer(inputs, w_qkv, norm_gain, w_out):
    parts = lax.axis_size("head")
    total = lax.axis_size("seq")
    seq = lax.axis_index("seq")
    core = lax.rem(seq, 2)
    y = lax.rem(seq // 2, 4)
    x = seq // 8
    head = lax.axis_index("head")
    core_id = core.astype(jnp.int32).reshape(1)
    place = [a.astype(jnp.int32).reshape(1) for a in (head, core, y, x)]

    def along(direction):
        pairs = []
        for i in range(total):
            shift = direction * (1 - 2 * (i % 2))
            for h in range(parts):
                pairs.append((i * parts + h, i * parts + (h + shift) % parts))
        return pairs

    partner = [(i, i ^ 1) for i in range(total)]

    def swap(a):
        return lax.ppermute(a, "seq", partner)

    def send(a, direction):
        return lax.ppermute(a, ("seq", "head"), along(direction))

    near = send(w_out, 1)
    rows = w_out.shape[0] // 2
    far = lax.dynamic_slice_in_dim(near, core * rows, rows, 0)
    far = send(far, 1)
    near_other = swap(near)
    far_other = swap(far)

    q, k, v, pre, tot, att = project(inputs, w_qkv, 1)
    other = swap(tot)
    for piece in range(1, 4):
        att = local_part(q, k, v, pre, att, piece, 4)
    y1, y2, row = pair_rounds(tot.astype(F32) + other.astype(F32), 2, total)
    x1, x2, _ = pair_rounds(row, 8, total)
    received = (other, y1, y2, x1, x2)

    gain = norm_gain.reshape(1, -1)
    nf, pair = finish(place, 0, 2, q, att, received, gain, parts)
    nf = send(nf, 1)
    na = send(finish(place, 1, 0, q, att, (pair,), gain, parts), 1)
    nb = send(finish(place, -1, 0, q, att, (pair,), gain, parts), -1)
    nf = send(nf, 1)
    n0 = finish(place, 0, 0, q, att, (pair,), gain, parts)
    acc, near, *weights = mix_own(n0, w_out, [near, near_other, far, far_other])
    acc = mix_middle(acc, na, near)
    return mix_last(core_id, acc, [nb, nf], weights)


def solution(mesh):
    return jax.shard_map(
        layer,
        mesh=mesh,
        in_specs=(P("seq", None), P(None, None, "head"), P("head"), P("head", None)),
        out_specs=P(("seq", "head"), None),
        check_vma=False,
    )
```

```python
import jax
import jax.numpy as jnp
from jax import lax
from jax.experimental import pallas as pl
from jax.experimental.pallas import tpu as pltpu
from jax.sharding import PartitionSpec as P


DH = 128
BLK = 256
F32 = jnp.float32
BF16 = jnp.bfloat16


def dot(a, b):
    return jnp.dot(a, b, preferred_element_type=F32)


def cost(flops, nbytes):
    return pl.CostEstimate(flops=int(flops), bytes_accessed=int(nbytes), transcendentals=0)


def hi_lo(state):
    high = state.astype(BF16)
    low = (state - high.astype(F32)).astype(BF16)
    return jnp.concatenate([high, low], axis=0)


def local_block(att_ref, rows, q_ref, k_ref, v_ref, pre, at):
    lower = lax.broadcasted_iota(jnp.int32, (BLK, BLK), 0) >= lax.broadcasted_iota(
        jnp.int32, (BLK, BLK), 1
    )
    for h in range(q_ref.shape[1] // DH):
        cols = slice(h * DH, (h + 1) * DH)
        q = q_ref[rows, cols]
        scores = lax.dot_general(
            q, k_ref[rows, cols], (((1,), (1,)), ((), ())), preferred_element_type=F32
        )
        scores = jnp.where(lower, scores, 0.0).astype(BF16)
        att_ref[rows, cols] = dot(scores, v_ref[rows, cols]) + dot(
            jnp.concatenate([q, q], axis=1), pre[at, h]
        )


def qkv_kernel(
    x_hbm, w_hbm, q_hbm, k_hbm, v_hbm, pre_hbm, tot_ref, att_hbm,
    x, w, q, k, v, pre, att, x_sem, w_sem, out_sem,
):
    steps = x_sem.shape[0] // 2
    tile = x.shape[0] // steps
    width = x.shape[1]
    half = width // 2
    heads = tot_ref.shape[0]
    blocks = tile // BLK
    inside = att.shape[0] // tile

    def tokens(i, part):
        at = (pl.ds(i * tile, tile), pl.ds(part * half, half))
        return pltpu.make_async_copy(x_hbm.at[at], x.at[at], x_sem.at[2 * i + part])

    def weight(which, part):
        at = pl.ds(part * half, half)
        return pltpu.make_async_copy(
            w_hbm.at[which, at], w.at[which, at], w_sem.at[2 * which + part]
        )

    for part in range(2):
        tokens(0, part).start()
        weight(1, part).start()
    for which in (2, 0):
        for part in range(2):
            weight(which, part).start()
    for i in range(1, steps):
        for part in range(2):
            tokens(i, part).start()

    pending = []

    def put(i, source, target, which):
        copy = pltpu.make_async_copy(source, target, out_sem.at[i, which])
        copy.start()
        pending.append(copy)

    state = [jnp.zeros((DH, DH), F32)] * heads
    for i in range(steps):
        rows = pl.ds(i * tile, tile)
        if i == 0:
            total = None
            for part in range(2):
                tokens(0, part).wait()
                weight(1, part).wait()
                cut = pl.ds(part * half, half)
                product = dot(x[rows, cut], w[1, cut])
                total = product if total is None else total + product
            k[rows] = total.astype(BF16)
        else:
            for part in range(2):
                tokens(i, part).wait()
            k[rows] = dot(x[rows], w[1]).astype(BF16)
        for which, out in ((2, v), (0, q)):
            if i == 0:
                for part in range(2):
                    weight(which, part).wait()
            out[rows] = dot(x[rows], w[which]).astype(BF16)
        for b in range(i * blocks, (i + 1) * blocks):
            block = slice(b * BLK, (b + 1) * BLK)
            for h in range(heads):
                cols = slice(h * DH, (h + 1) * DH)
                pre[b, h] = hi_lo(state[h])
                state[h] = state[h] + lax.dot_general(
                    k[block, cols], v[block, cols], (((0,), (0,)), ((), ())),
                    preferred_element_type=F32,
                )
            if i < inside:
                local_block(att, block, q, k, v, pre, b)
        put(i, q.at[rows], q_hbm.at[rows], 0)
        put(i, k.at[rows], k_hbm.at[rows], 1)
        put(i, v.at[rows], v_hbm.at[rows], 2)
        at = pl.ds(i * blocks, blocks)
        put(i, pre.at[at], pre_hbm.at[at], 3)
        if i < inside:
            put(i, att.at[rows], att_hbm.at[rows], 4)
    for h in range(heads):
        tot_ref[h] = state[h].astype(BF16)
    for copy in pending:
        copy.wait()


def project(x, w_qkv, inside, tile=512):
    tokens, width = x.shape
    feats = w_qkv.shape[2]
    heads = feats // DH
    steps = tokens // tile
    wide = (tokens, feats)
    states = (tokens // BLK, heads, 2 * DH, DH)
    anywhere = pl.BlockSpec(memory_space=pl.ANY)
    return pl.pallas_call(
        qkv_kernel,
        in_specs=[anywhere] * 2,
        out_specs=[anywhere] * 4 + [pl.BlockSpec(memory_space=pltpu.VMEM), anywhere],
        out_shape=[jax.ShapeDtypeStruct(wide, BF16)] * 3
        + [
            jax.ShapeDtypeStruct(states, BF16),
            jax.ShapeDtypeStruct((heads, DH, DH), BF16),
            jax.ShapeDtypeStruct(wide, F32),
        ],
        scratch_shapes=[
            pltpu.VMEM((tokens, width), BF16),
            pltpu.VMEM((3, width, feats), BF16),
            pltpu.VMEM(wide, BF16),
            pltpu.VMEM(wide, BF16),
            pltpu.VMEM(wide, BF16),
            pltpu.VMEM(states, BF16),
            pltpu.VMEM((inside * tile, feats), F32),
            pltpu.SemaphoreType.DMA((2 * steps,)),
            pltpu.SemaphoreType.DMA((6,)),
            pltpu.SemaphoreType.DMA((steps, 5)),
        ],
        cost_estimate=cost(6 * tokens * width * feats, 2 * tokens * width + 6 * width * feats),
        name="project",
    )(x, w_qkv)


def local_kernel(q_ref, k_ref, v_ref, pre_ref, att_in, att_ref):
    for b in range(q_ref.shape[0] // BLK):
        local_block(att_ref, slice(b * BLK, (b + 1) * BLK), q_ref, k_ref, v_ref, pre_ref, b)


def local_part(q, k, v, pre, att, piece, pieces, tile=256):
    tokens, feats = q.shape
    heads = feats // DH
    blocks = tile // BLK
    count = tokens // pieces
    start = piece * count // tile
    row = pl.BlockSpec((tile, feats), lambda i: (i + start, 0))
    return pl.pallas_call(
        local_kernel,
        grid=(count // tile,),
        in_specs=[
            row, row, row,
            pl.BlockSpec((blocks, heads, 2 * DH, DH), lambda i: (i + start, 0, 0, 0)),
            pl.BlockSpec(memory_space=pl.ANY),
        ],
        out_specs=row,
        out_shape=jax.ShapeDtypeStruct((tokens, feats), F32),
        input_output_aliases={4: 0},
        cost_estimate=cost(8 * count * feats * BLK, 14 * count * feats),
        name="local_part",
    )(q, k, v, pre, att)


def norm_rows(q_ref, att_ref, pair, gain_ref, n_ref, h):
    cols = slice(h * DH, (h + 1) * DH)
    q = q_ref[:, cols]
    att = att_ref[:, cols] + dot(jnp.concatenate([q, q], axis=1), pair)
    mean_sq = jnp.mean(att * att, axis=-1, keepdims=True)
    n_ref[:, cols] = (att * lax.rsqrt(mean_sq + 1e-06) * gain_ref[:, cols]).astype(BF16)


def start_kernel(
    head, core, q_ref, att_ref, core_ref, mine_ref, partner_ref, gain_ref, n_ref, pair_ref
):
    heads = core_ref.shape[0]
    half = heads // 2
    for h in range(heads):

        @pl.when(pl.program_id(0) == 0)
        def _():
            carried = jnp.where(core[0] == 1, core_ref[h].astype(F32), 0.0)
            carried = carried + jnp.where(
                core[0] == h // half, mine_ref[h % half], partner_ref[h % half]
            )
            pair_ref[h] = hi_lo(carried)

    for h in range(heads):
        norm_rows(q_ref, att_ref, pair_ref[h], gain_ref, n_ref, h)


def finish_kernel(head, core, q_ref, att_ref, pair_ref, gain_ref, n_ref):
    for h in range(pair_ref.shape[0]):
        norm_rows(q_ref, att_ref, pair_ref[h], gain_ref, n_ref, h)


def finish(place, direction, shift, q, att, received, gain, parts, tile=256):
    tokens, feats = q.shape
    count = tokens // parts
    per = count // tile
    heads = feats // DH

    def row(i, head, core):
        to = head[0] + direction * (1 - 2 * core[0]) + shift + parts
        return (lax.rem(to, parts) * per + i, 0)

    first = len(received) > 1
    normed = jax.ShapeDtypeStruct((count, feats), BF16)
    rows = pl.BlockSpec((tile, feats), lambda i, *place: (i, 0))
    whole = lambda a: pl.BlockSpec(a.shape, lambda i, *place: (0,) * len(a.shape))
    pair = jax.ShapeDtypeStruct((heads, 2 * DH, DH), BF16)
    return pl.pallas_call(
        start_kernel if first else finish_kernel,
        grid_spec=pltpu.PrefetchScalarGridSpec(
            num_scalar_prefetch=2,
            grid=(per,),
            in_specs=[pl.BlockSpec((tile, feats), row), pl.BlockSpec((tile, feats), row)]
            + [whole(a) for a in received]
            + [whole(gain)],
            out_specs=[rows, whole(pair)] if first else rows,
        ),
        out_shape=[normed, pair] if first else normed,
        cost_estimate=cost(2 * count * feats * DH * 2, count * feats * 8),
        name="finish",
    )(*place, q, att, *received, gain)


def own_kernel(n_ref, w_ref, *rest):
    later, (acc_ref, *passed, sem) = rest[: len(rest) // 2 - 1], rest[len(rest) // 2 - 1 :]
    copies = [
        pltpu.make_async_copy(source, target, sem.at[i])
        for i, (source, target) in enumerate(zip(later, passed))
    ]

    @pl.when(pl.program_id(0) == 0)
    def _():
        for copy in copies:
            copy.start()

    acc_ref[...] = dot(n_ref[...], w_ref[...])

    @pl.when(pl.program_id(0) == pl.num_programs(0) - 1)
    def _():
        for copy in copies:
            copy.wait()


def mix_own(normed, weight, later, tile=512):
    rows, feats = normed.shape
    width = weight.shape[1]
    anywhere = [pl.BlockSpec(memory_space=pl.ANY)] * len(later)
    return pl.pallas_call(
        own_kernel,
        grid=(width // tile,),
        in_specs=[
            pl.BlockSpec((rows, feats), lambda i: (0, 0)),
            pl.BlockSpec((feats, tile), lambda i: (0, i)),
        ]
        + anywhere,
        out_specs=[pl.BlockSpec((rows, tile), lambda i: (0, i))] + anywhere,
        out_shape=[jax.ShapeDtypeStruct((rows, width), F32)]
        + [jax.ShapeDtypeStruct(a.shape, a.dtype) for a in later],
        scratch_shapes=[pltpu.SemaphoreType.DMA((len(later),))],
        cost_estimate=cost(2 * rows * feats * width, 8 * rows * width),
        compiler_params=pltpu.CompilerParams(vmem_limit_bytes=24 << 20),
        name="mix_own",
    )(normed, weight, *later)


def middle_kernel(acc_ref, n_ref, w_ref, out_ref):
    out_ref[...] = acc_ref[...] + dot(n_ref[...], w_ref[...])


def mix_middle(acc, normed, weight, tile=512):
    rows, feats = normed.shape
    width = acc.shape[1]
    column = lambda a: pl.BlockSpec((a.shape[0], tile), lambda i: (0, i))
    return pl.pallas_call(
        middle_kernel,
        grid=(width // tile,),
        in_specs=[column(acc), pl.BlockSpec((rows, feats), lambda i: (0, 0)), column(weight)],
        out_specs=column(acc),
        out_shape=jax.ShapeDtypeStruct((rows, width), F32),
        input_output_aliases={0: 0},
        cost_estimate=cost(2 * rows * feats * width, 8 * rows * width),
        compiler_params=pltpu.CompilerParams(vmem_limit_bytes=24 << 20),
        name="mix_middle",
    )(acc, normed, weight)


def last_kernel(core, acc_ref, nb, nf, wb, mine_ref, other_ref, out_ref):
    half = mine_ref.shape[0]
    mine = pl.multiple_of(core[0] * half, half)
    other = pl.multiple_of((1 - core[0]) * half, half)
    acc = dot(nb[...], wb[...])
    acc += dot(nf[:, pl.ds(mine, half)], mine_ref[...])
    acc += dot(nf[:, pl.ds(other, half)], other_ref[...])
    out_ref[...] = (acc + acc_ref[...]).astype(BF16)


def mix_last(core, acc, normed, weights, tile=512):
    rows, feats = normed[0].shape
    width = acc.shape[1]
    column = lambda a: pl.BlockSpec((a.shape[0], tile), lambda i, core: (0, i))
    return pl.pallas_call(
        last_kernel,
        grid_spec=pltpu.PrefetchScalarGridSpec(
            num_scalar_prefetch=1,
            grid=(width // tile,),
            in_specs=[column(acc)]
            + [pl.BlockSpec(a.shape, lambda i, core: (0, 0)) for a in normed]
            + [column(a) for a in weights],
            out_specs=pl.BlockSpec((rows, tile), lambda i, core: (0, i)),
        ),
        out_shape=jax.ShapeDtypeStruct((rows, width), BF16),
        cost_estimate=cost(4 * rows * feats * width, 8 * rows * width),
        compiler_params=pltpu.CompilerParams(vmem_limit_bytes=24 << 20),
        name="mix_last",
    )(core, acc, *normed, *weights)


def pair_up(size, stride, total, first):
    pairs = []
    for i in range(total):
        at = (i // stride) % size
        to = at ^ 1 if first else (at + (1 if at % 2 else -1)) % size
        pairs.append((i, i + (to - at) * stride))
    return pairs


def pair_rounds(value, stride, total):
    value = value.astype(BF16)
    other = lax.ppermute(value, "seq", pair_up(4, stride, total, True))
    pair = (value.astype(F32) + other.astype(F32)).astype(BF16)
    far = lax.ppermute(pair, "seq", pair_up(4, stride, total, False))
    return other, far, pair.astype(F32) + far.astype(F32)


def layer(inputs, w_qkv, norm_gain, w_out):
    parts = lax.axis_size("head")
    total = lax.axis_size("seq")
    seq = lax.axis_index("seq")
    core = lax.rem(seq, 2)
    y = lax.rem(seq // 2, 4)
    x = seq // 8
    head = lax.axis_index("head")
    core_id = core.astype(jnp.int32).reshape(1)
    place = [a.astype(jnp.int32).reshape(1) for a in (head, core)]

    def along(direction):
        pairs = []
        for i in range(total):
            shift = direction * (1 - 2 * (i % 2))
            for h in range(parts):
                pairs.append((i * parts + h, i * parts + (h + shift) % parts))
        return pairs

    partner = [(i, i ^ 1) for i in range(total)]

    def swap(a):
        return lax.ppermute(a, "seq", partner)

    def send(a, direction):
        return lax.ppermute(a, ("seq", "head"), along(direction))

    near = send(w_out, 1)
    rows = w_out.shape[0] // 2
    far = lax.dynamic_slice_in_dim(near, core * rows, rows, 0)
    far = send(far, 1)
    near_other = swap(near)
    far_other = swap(far)

    q, k, v, pre, tot, att = project(inputs, w_qkv, 1)
    other = swap(tot)
    for piece in range(1, 4):
        att = local_part(q, k, v, pre, att, piece, 4)
    chip = tot.astype(F32) + other.astype(F32)
    half = chip.shape[0] // 2
    chip = lax.dynamic_slice_in_dim(chip, core * half, half, 0)
    y1, y2, row = pair_rounds(chip, 2, total)
    x1, x2, _ = pair_rounds(row, 8, total)
    takes = (
        (lax.rem(y, 2) == 1, y1),
        (y >= 2, y2),
        (lax.rem(x, 2) == 1, x1),
        (x >= 2, x2),
    )
    mine = sum(jnp.where(take, part.astype(F32), 0.0) for take, part in takes)
    received = (other, mine, swap(mine))

    gain = norm_gain.reshape(1, -1)
    nf, pair = finish(place, 0, 2, q, att, received, gain, parts)
    nf = send(nf, 1)
    na = send(finish(place, 1, 0, q, att, (pair,), gain, parts), 1)
    nb = send(finish(place, -1, 0, q, att, (pair,), gain, parts), -1)
    nf = send(nf, 1)
    n0 = finish(place, 0, 0, q, att, (pair,), gain, parts)
    acc, near, *weights = mix_own(n0, w_out, [near, near_other, far, far_other])
    acc = mix_middle(acc, na, near)
    return mix_last(core_id, acc, [nb, nf], weights)


def solution(mesh):
    return jax.shard_map(
        layer,
        mesh=mesh,
        in_specs=(P("seq", None), P(None, None, "head"), P("head"), P("head", None)),
        out_specs=P(("seq", "head"), None),
        check_vma=False,
    )
```

```python
import jax
import jax.numpy as jnp
from jax import lax
from jax.experimental import pallas as pl
from jax.experimental.pallas import tpu as pltpu
from jax.sharding import PartitionSpec as P


DH = 128
BLK = 256
F32 = jnp.float32
BF16 = jnp.bfloat16


def dot(a, b):
    return jnp.dot(a, b, preferred_element_type=F32)


def cost(flops, nbytes):
    return pl.CostEstimate(flops=int(flops), bytes_accessed=int(nbytes), transcendentals=0)


def hi_lo(state):
    high = state.astype(BF16)
    low = (state - high.astype(F32)).astype(BF16)
    return jnp.concatenate([high, low], axis=0)


def local_block(att_ref, rows, q_ref, k_ref, v_ref, pre, at):
    lower = lax.broadcasted_iota(jnp.int32, (BLK, BLK), 0) >= lax.broadcasted_iota(
        jnp.int32, (BLK, BLK), 1
    )
    for h in range(q_ref.shape[1] // DH):
        cols = slice(h * DH, (h + 1) * DH)
        q = q_ref[rows, cols]
        scores = lax.dot_general(
            q, k_ref[rows, cols], (((1,), (1,)), ((), ())), preferred_element_type=F32
        )
        scores = jnp.where(lower, scores, 0.0).astype(BF16)
        att_ref[rows, cols] = dot(scores, v_ref[rows, cols]) + dot(
            jnp.concatenate([q, q], axis=1), pre[at, h]
        )


def qkv_kernel(
    x_hbm, w_hbm, qkv_hbm, pre_hbm, tot_ref, att_hbm,
    x, w, qkv, pre, att, x_sem, w_sem, out_sem,
):
    steps = x_sem.shape[0] - 1
    tile = x.shape[0] // steps
    half = x.shape[1] // 2
    heads = tot_ref.shape[0]
    blocks = tile // BLK
    inside = att.shape[0] // tile
    q, k, v = (qkv.at[which] for which in range(3))

    firsts = []
    for part in range(2):
        cut = pl.ds(part * half, half)
        at = (pl.ds(0, tile), cut)
        firsts.append(
            (
                pltpu.make_async_copy(x_hbm.at[at], x.at[at], x_sem.at[part]),
                pltpu.make_async_copy(w_hbm.at[1, cut], w.at[1, cut], w_sem.at[part]),
            )
        )
    weights = {
        which: pltpu.make_async_copy(w_hbm.at[which], w.at[which], w_sem.at[2 + at])
        for at, which in enumerate((2, 0))
    }
    tokens = []
    for i in range(1, steps):
        at = pl.ds(i * tile, tile)
        tokens.append(pltpu.make_async_copy(x_hbm.at[at], x.at[at], x_sem.at[1 + i]))
    for copies in firsts:
        for copy in copies:
            copy.start()
    for copy in (*weights.values(), *tokens):
        copy.start()

    pending = []

    def put(source, target):
        copy = pltpu.make_async_copy(source, target, out_sem.at[len(pending)])
        copy.start()
        pending.append(copy)

    state = [jnp.zeros((DH, DH), F32)] * heads
    for i in range(steps):
        rows = pl.ds(i * tile, tile)
        if i == 0:
            total = None
            for part, copies in enumerate(firsts):
                for copy in copies:
                    copy.wait()
                cut = pl.ds(part * half, half)
                product = dot(x[rows, cut], w[1, cut])
                total = product if total is None else total + product
            k[rows] = total.astype(BF16)
        else:
            tokens[i - 1].wait()
            k[rows] = dot(x[rows], w[1]).astype(BF16)
        for which, out in ((2, v), (0, q)):
            if i == 0:
                weights[which].wait()
            out[rows] = dot(x[rows], w[which]).astype(BF16)
        for b in range(i * blocks, (i + 1) * blocks):
            block = slice(b * BLK, (b + 1) * BLK)
            for h in range(heads):
                cols = slice(h * DH, (h + 1) * DH)
                pre[b, h] = hi_lo(state[h])
                state[h] = state[h] + lax.dot_general(
                    k[block, cols], v[block, cols], (((0,), (0,)), ((), ())),
                    preferred_element_type=F32,
                )
            if i < inside:
                local_block(att, block, q, k, v, pre, b)
        put(qkv.at[:, rows], qkv_hbm.at[:, rows])
        at = pl.ds(i * blocks, blocks)
        put(pre.at[at], pre_hbm.at[at])
        if i == inside - 1:
            at = pl.ds(0, inside * tile)
            put(att, att_hbm.at[at])
    for h in range(heads):
        tot_ref[h] = state[h].astype(BF16)
    for copy in pending:
        copy.wait()


def project(x, w_qkv, inside, tile=512):
    tokens, width = x.shape
    feats = w_qkv.shape[2]
    heads = feats // DH
    steps = tokens // tile
    wide = (tokens, feats)
    states = (tokens // BLK, heads, 2 * DH, DH)
    anywhere = pl.BlockSpec(memory_space=pl.ANY)
    return pl.pallas_call(
        qkv_kernel,
        in_specs=[anywhere] * 2,
        out_specs=[anywhere] * 2 + [pl.BlockSpec(memory_space=pltpu.VMEM), anywhere],
        out_shape=[
            jax.ShapeDtypeStruct((3, *wide), BF16),
            jax.ShapeDtypeStruct(states, BF16),
            jax.ShapeDtypeStruct((heads, DH, DH), BF16),
            jax.ShapeDtypeStruct(wide, F32),
        ],
        scratch_shapes=[
            pltpu.VMEM((tokens, width), BF16),
            pltpu.VMEM((3, width, feats), BF16),
            pltpu.VMEM((3, *wide), BF16),
            pltpu.VMEM(states, BF16),
            pltpu.VMEM((inside * tile, feats), F32),
            pltpu.SemaphoreType.DMA((steps + 1,)),
            pltpu.SemaphoreType.DMA((4,)),
            pltpu.SemaphoreType.DMA((2 * steps + 1,)),
        ],
        cost_estimate=cost(6 * tokens * width * feats, 2 * tokens * width + 6 * width * feats),
        name="project",
    )(x, w_qkv)


def local_kernel(q_ref, k_ref, v_ref, pre_ref, att_in, att_ref):
    for b in range(q_ref.shape[0] // BLK):
        local_block(att_ref, slice(b * BLK, (b + 1) * BLK), q_ref, k_ref, v_ref, pre_ref, b)


def local_part(qkv, pre, att, piece, pieces, tile=256):
    _, tokens, feats = qkv.shape
    heads = feats // DH
    blocks = tile // BLK
    count = tokens // pieces
    start = piece * count // tile
    row = pl.BlockSpec((tile, feats), lambda i: (i + start, 0))
    part = lambda which: pl.BlockSpec((None, tile, feats), lambda i: (which, i + start, 0))
    return pl.pallas_call(
        local_kernel,
        grid=(count // tile,),
        in_specs=[
            part(0), part(1), part(2),
            pl.BlockSpec((blocks, heads, 2 * DH, DH), lambda i: (i + start, 0, 0, 0)),
            pl.BlockSpec(memory_space=pl.ANY),
        ],
        out_specs=row,
        out_shape=jax.ShapeDtypeStruct((tokens, feats), F32),
        input_output_aliases={4: 0},
        cost_estimate=cost(8 * count * feats * BLK, 14 * count * feats),
        name="local_part",
    )(qkv, qkv, qkv, pre, att)


def norm_rows(q_ref, att_ref, pair, gain_ref, n_ref, h):
    cols = slice(h * DH, (h + 1) * DH)
    q = q_ref[:, cols]
    att = att_ref[:, cols] + dot(jnp.concatenate([q, q], axis=1), pair)
    mean_sq = jnp.mean(att * att, axis=-1, keepdims=True)
    n_ref[:, cols] = (att * lax.rsqrt(mean_sq + 1e-06) * gain_ref[:, cols]).astype(BF16)


def start_kernel(
    head, core, q_ref, att_ref, core_ref, mine_ref, partner_ref, gain_ref, n_ref, pair_ref
):
    heads = core_ref.shape[0]
    half = heads // 2
    for h in range(heads):

        @pl.when(pl.program_id(0) == 0)
        def _():
            carried = jnp.where(core[0] == 1, core_ref[h].astype(F32), 0.0)
            carried = carried + jnp.where(
                core[0] == h // half, mine_ref[h % half], partner_ref[h % half]
            )
            pair_ref[h] = hi_lo(carried)

    for h in range(heads):
        norm_rows(q_ref, att_ref, pair_ref[h], gain_ref, n_ref, h)


def finish_kernel(head, core, q_ref, att_ref, pair_ref, gain_ref, n_ref):
    for h in range(pair_ref.shape[0]):
        norm_rows(q_ref, att_ref, pair_ref[h], gain_ref, n_ref, h)


def finish(place, direction, shift, qkv, att, received, gain, parts, tile=256):
    _, tokens, feats = qkv.shape
    count = tokens // parts
    per = count // tile
    heads = feats // DH

    def row(i, head, core):
        to = head[0] + direction * (1 - 2 * core[0]) + shift + parts
        return (lax.rem(to, parts) * per + i, 0)

    first = len(received) > 1
    normed = jax.ShapeDtypeStruct((count, feats), BF16)
    rows = pl.BlockSpec((tile, feats), lambda i, *place: (i, 0))
    whole = lambda a: pl.BlockSpec(a.shape, lambda i, *place: (0,) * len(a.shape))
    pair = jax.ShapeDtypeStruct((heads, 2 * DH, DH), BF16)
    return pl.pallas_call(
        start_kernel if first else finish_kernel,
        grid_spec=pltpu.PrefetchScalarGridSpec(
            num_scalar_prefetch=2,
            grid=(per,),
            in_specs=[
                pl.BlockSpec((None, tile, feats), lambda *at: (0, *row(*at))),
                pl.BlockSpec((tile, feats), row),
            ]
            + [whole(a) for a in received]
            + [whole(gain)],
            out_specs=[rows, whole(pair)] if first else rows,
        ),
        out_shape=[normed, pair] if first else normed,
        cost_estimate=cost(2 * count * feats * DH * 2, count * feats * 8),
        name="finish",
    )(*place, qkv, att, *received, gain)


def own_kernel(n_ref, w_ref, *rest):
    later, (acc_ref, *passed, sem) = rest[: len(rest) // 2 - 1], rest[len(rest) // 2 - 1 :]
    copies = [
        pltpu.make_async_copy(source, target, sem.at[i])
        for i, (source, target) in enumerate(zip(later, passed))
    ]

    @pl.when(pl.program_id(0) == 0)
    def _():
        for copy in copies:
            copy.start()

    acc_ref[...] = dot(n_ref[...], w_ref[...])

    @pl.when(pl.program_id(0) == pl.num_programs(0) - 1)
    def _():
        for copy in copies:
            copy.wait()


def mix_own(normed, weight, later, tile=512):
    rows, feats = normed.shape
    width = weight.shape[1]
    anywhere = [pl.BlockSpec(memory_space=pl.ANY)] * len(later)
    return pl.pallas_call(
        own_kernel,
        grid=(width // tile,),
        in_specs=[
            pl.BlockSpec((rows, feats), lambda i: (0, 0)),
            pl.BlockSpec((feats, tile), lambda i: (0, i)),
        ]
        + anywhere,
        out_specs=[pl.BlockSpec((rows, tile), lambda i: (0, i))] + anywhere,
        out_shape=[jax.ShapeDtypeStruct((rows, width), F32)]
        + [jax.ShapeDtypeStruct(a.shape, a.dtype) for a in later],
        scratch_shapes=[pltpu.SemaphoreType.DMA((len(later),))],
        cost_estimate=cost(2 * rows * feats * width, 8 * rows * width),
        compiler_params=pltpu.CompilerParams(vmem_limit_bytes=24 << 20),
        name="mix_own",
    )(normed, weight, *later)


def middle_kernel(acc_ref, n_ref, w_ref, out_ref):
    out_ref[...] = acc_ref[...] + dot(n_ref[...], w_ref[...])


def mix_middle(acc, normed, weight, tile=512):
    rows, feats = normed.shape
    width = acc.shape[1]
    column = lambda a: pl.BlockSpec((a.shape[0], tile), lambda i: (0, i))
    return pl.pallas_call(
        middle_kernel,
        grid=(width // tile,),
        in_specs=[column(acc), pl.BlockSpec((rows, feats), lambda i: (0, 0)), column(weight)],
        out_specs=column(acc),
        out_shape=jax.ShapeDtypeStruct((rows, width), F32),
        input_output_aliases={0: 0},
        cost_estimate=cost(2 * rows * feats * width, 8 * rows * width),
        compiler_params=pltpu.CompilerParams(vmem_limit_bytes=24 << 20),
        name="mix_middle",
    )(acc, normed, weight)


def last_kernel(core, acc_ref, nf, mine_ref, other_ref, out_ref):
    half = mine_ref.shape[0]
    mine = pl.multiple_of(core[0] * half, half)
    other = pl.multiple_of((1 - core[0]) * half, half)
    acc = dot(nf[:, pl.ds(mine, half)], mine_ref[...])
    acc += dot(nf[:, pl.ds(other, half)], other_ref[...])
    out_ref[...] = (acc + acc_ref[...]).astype(BF16)


def mix_last(core, acc, normed, weights, tile=512):
    rows, feats = normed[0].shape
    width = acc.shape[1]
    column = lambda a: pl.BlockSpec((a.shape[0], tile), lambda i, core: (0, i))
    return pl.pallas_call(
        last_kernel,
        grid_spec=pltpu.PrefetchScalarGridSpec(
            num_scalar_prefetch=1,
            grid=(width // tile,),
            in_specs=[column(acc)]
            + [pl.BlockSpec(a.shape, lambda i, core: (0, 0)) for a in normed]
            + [column(a) for a in weights],
            out_specs=pl.BlockSpec((rows, tile), lambda i, core: (0, i)),
        ),
        out_shape=jax.ShapeDtypeStruct((rows, width), BF16),
        cost_estimate=cost(2 * rows * feats * width, 8 * rows * width),
        compiler_params=pltpu.CompilerParams(vmem_limit_bytes=24 << 20),
        name="mix_last",
    )(core, acc, *normed, *weights)


def pair_up(size, stride, total, first):
    pairs = []
    for i in range(total):
        at = (i // stride) % size
        to = at ^ 1 if first else (at + (1 if at % 2 else -1)) % size
        pairs.append((i, i + (to - at) * stride))
    return pairs


def pair_rounds(value, stride, total):
    value = value.astype(BF16)
    other = lax.ppermute(value, "seq", pair_up(4, stride, total, True))
    pair = (value.astype(F32) + other.astype(F32)).astype(BF16)
    far = lax.ppermute(pair, "seq", pair_up(4, stride, total, False))
    return other, far, pair.astype(F32) + far.astype(F32)


def layer(inputs, w_qkv, norm_gain, w_out):
    parts = lax.axis_size("head")
    total = lax.axis_size("seq")
    seq = lax.axis_index("seq")
    core = lax.rem(seq, 2)
    y = lax.rem(seq // 2, 4)
    x = seq // 8
    head = lax.axis_index("head")
    core_id = core.astype(jnp.int32).reshape(1)
    place = [a.astype(jnp.int32).reshape(1) for a in (head, core)]

    def along(direction):
        pairs = []
        for i in range(total):
            shift = direction * (1 - 2 * (i % 2))
            for h in range(parts):
                pairs.append((i * parts + h, i * parts + (h + shift) % parts))
        return pairs

    partner = [(i, i ^ 1) for i in range(total)]

    def swap(a):
        return lax.ppermute(a, "seq", partner)

    def send(a, direction):
        return lax.ppermute(a, ("seq", "head"), along(direction))

    near = send(w_out, 1)
    rows = w_out.shape[0] // 2
    far = lax.dynamic_slice_in_dim(near, core * rows, rows, 0)
    far = send(far, 1)
    near_other = swap(near)
    far_other = swap(far)

    qkv, pre, tot, att = project(inputs, w_qkv, 1)
    other = swap(tot)
    for piece in range(1, 4):
        att = local_part(qkv, pre, att, piece, 4)
    chip = tot.astype(F32) + other.astype(F32)
    half = chip.shape[0] // 2
    chip = lax.dynamic_slice_in_dim(chip, core * half, half, 0)
    y1, y2, row = pair_rounds(chip, 2, total)
    x1, x2, _ = pair_rounds(row, 8, total)
    takes = (
        (lax.rem(y, 2) == 1, y1),
        (y >= 2, y2),
        (lax.rem(x, 2) == 1, x1),
        (x >= 2, x2),
    )
    mine = sum(jnp.where(take, part.astype(F32), 0.0) for take, part in takes)
    received = (other, mine, swap(mine))

    gain = norm_gain.reshape(1, -1)
    nf, pair = finish(place, 0, 2, qkv, att, received, gain, parts)
    nf = send(nf, 1)
    na = send(finish(place, 1, 0, qkv, att, (pair,), gain, parts), 1)
    nb = send(finish(place, -1, 0, qkv, att, (pair,), gain, parts), -1)
    nf = send(nf, 1)
    n0 = finish(place, 0, 0, qkv, att, (pair,), gain, parts)
    acc, near, near_other, *weights = mix_own(n0, w_out, [near, near_other, far, far_other])
    acc = mix_middle(acc, na, near)
    acc = mix_middle(acc, nb, near_other)
    return mix_last(core_id, acc, [nf], weights)


def solution(mesh):
    return jax.shard_map(
        layer,
        mesh=mesh,
        in_specs=(P("seq", None), P(None, None, "head"), P("head"), P("head", None)),
        out_specs=P(("seq", "head"), None),
        check_vma=False,
    )
```

```python
import jax
import jax.numpy as jnp
from jax import lax
from jax.experimental import pallas as pl
from jax.experimental.pallas import tpu as pltpu
from jax.sharding import PartitionSpec as P


DH = 128
BLK = 256
F32 = jnp.float32
BF16 = jnp.bfloat16


def dot(a, b):
    return jnp.dot(a, b, preferred_element_type=F32)


def cost(flops, nbytes):
    return pl.CostEstimate(flops=int(flops), bytes_accessed=int(nbytes), transcendentals=0)


def hi_lo(state):
    high = state.astype(BF16)
    low = (state - high.astype(F32)).astype(BF16)
    return jnp.concatenate([high, low], axis=0)


def local_block(att_ref, rows, q_ref, k_ref, v_ref, pre, at):
    lower = lax.broadcasted_iota(jnp.int32, (BLK, BLK), 0) >= lax.broadcasted_iota(
        jnp.int32, (BLK, BLK), 1
    )
    for h in range(q_ref.shape[1] // DH):
        cols = slice(h * DH, (h + 1) * DH)
        q = q_ref[rows, cols]
        scores = lax.dot_general(
            q, k_ref[rows, cols], (((1,), (1,)), ((), ())), preferred_element_type=F32
        )
        scores = jnp.where(lower, scores, 0.0).astype(BF16)
        att_ref[rows, cols] = dot(scores, v_ref[rows, cols]) + dot(
            jnp.concatenate([q, q], axis=1), pre[at, h]
        )


def qkv_kernel(
    x_hbm, w_hbm, qkv_hbm, pre_hbm, tot_ref, att_hbm,
    x, w, qkv, pre, att, x_sem, w_sem, out_sem,
):
    cuts = w_sem.shape[0] - 2
    steps = x_sem.shape[0] - cuts + 1
    tile = x.shape[0] // steps
    depth = x.shape[1] // cuts
    heads = tot_ref.shape[0]
    blocks = tile // BLK
    inside = att.shape[0] // tile
    q, k, v = (qkv.at[which] for which in range(3))

    firsts = []
    for part in range(cuts):
        cut = pl.ds(part * depth, depth)
        at = (pl.ds(0, tile), cut)
        firsts.append(
            (
                pltpu.make_async_copy(x_hbm.at[at], x.at[at], x_sem.at[part]),
                pltpu.make_async_copy(w_hbm.at[1, cut], w.at[1, cut], w_sem.at[part]),
            )
        )
    weights = {
        which: pltpu.make_async_copy(w_hbm.at[which], w.at[which], w_sem.at[cuts + at])
        for at, which in enumerate((2, 0))
    }
    tokens = []
    for i in range(1, steps):
        at = pl.ds(i * tile, tile)
        tokens.append(pltpu.make_async_copy(x_hbm.at[at], x.at[at], x_sem.at[cuts - 1 + i]))
    for copies in firsts:
        for copy in copies:
            copy.start()
    for copy in (*weights.values(), *tokens):
        copy.start()

    pending = []

    def put(source, target):
        copy = pltpu.make_async_copy(source, target, out_sem.at[len(pending)])
        copy.start()
        pending.append(copy)

    state = [jnp.zeros((DH, DH), F32)] * heads
    for i in range(steps):
        rows = pl.ds(i * tile, tile)
        if i == 0:
            total = None
            for part, copies in enumerate(firsts):
                for copy in copies:
                    copy.wait()
                cut = pl.ds(part * depth, depth)
                product = dot(x[rows, cut], w[1, cut])
                total = product if total is None else total + product
            k[rows] = total.astype(BF16)
        else:
            tokens[i - 1].wait()
            k[rows] = dot(x[rows], w[1]).astype(BF16)
        for which, out in ((2, v), (0, q)):
            if i == 0:
                weights[which].wait()
            out[rows] = dot(x[rows], w[which]).astype(BF16)
        for b in range(i * blocks, (i + 1) * blocks):
            block = slice(b * BLK, (b + 1) * BLK)
            for h in range(heads):
                cols = slice(h * DH, (h + 1) * DH)
                pre[b, h] = hi_lo(state[h])
                state[h] = state[h] + lax.dot_general(
                    k[block, cols], v[block, cols], (((0,), (0,)), ((), ())),
                    preferred_element_type=F32,
                )
            if i < inside:
                local_block(att, block, q, k, v, pre, b)
        put(qkv.at[:, rows], qkv_hbm.at[:, rows])
        at = pl.ds(i * blocks, blocks)
        put(pre.at[at], pre_hbm.at[at])
        if i == inside - 1:
            at = pl.ds(0, inside * tile)
            put(att, att_hbm.at[at])
    for h in range(heads):
        tot_ref[h] = state[h].astype(BF16)
    for copy in pending:
        copy.wait()


def project(x, w_qkv, inside, tile=512, cuts=2):
    tokens, width = x.shape
    feats = w_qkv.shape[2]
    heads = feats // DH
    steps = tokens // tile
    wide = (tokens, feats)
    states = (tokens // BLK, heads, 2 * DH, DH)
    anywhere = pl.BlockSpec(memory_space=pl.ANY)
    return pl.pallas_call(
        qkv_kernel,
        in_specs=[anywhere] * 2,
        out_specs=[anywhere] * 2 + [pl.BlockSpec(memory_space=pltpu.VMEM), anywhere],
        out_shape=[
            jax.ShapeDtypeStruct((3, *wide), BF16),
            jax.ShapeDtypeStruct(states, BF16),
            jax.ShapeDtypeStruct((heads, DH, DH), BF16),
            jax.ShapeDtypeStruct(wide, F32),
        ],
        scratch_shapes=[
            pltpu.VMEM((tokens, width), BF16),
            pltpu.VMEM((3, width, feats), BF16),
            pltpu.VMEM((3, *wide), BF16),
            pltpu.VMEM(states, BF16),
            pltpu.VMEM((inside * tile, feats), F32),
            pltpu.SemaphoreType.DMA((steps - 1 + cuts,)),
            pltpu.SemaphoreType.DMA((2 + cuts,)),
            pltpu.SemaphoreType.DMA((2 * steps + 1,)),
        ],
        cost_estimate=cost(6 * tokens * width * feats, 2 * tokens * width + 6 * width * feats),
        name="project",
    )(x, w_qkv)


def local_kernel(q_ref, k_ref, v_ref, pre_ref, att_in, att_ref):
    for b in range(q_ref.shape[0] // BLK):
        local_block(att_ref, slice(b * BLK, (b + 1) * BLK), q_ref, k_ref, v_ref, pre_ref, b)


def local_part(qkv, pre, att, piece, pieces, tile=256):
    _, tokens, feats = qkv.shape
    heads = feats // DH
    blocks = tile // BLK
    count = tokens // pieces
    start = piece * count // tile
    row = pl.BlockSpec((tile, feats), lambda i: (i + start, 0))
    part = lambda which: pl.BlockSpec((None, tile, feats), lambda i: (which, i + start, 0))
    return pl.pallas_call(
        local_kernel,
        grid=(count // tile,),
        in_specs=[
            part(0), part(1), part(2),
            pl.BlockSpec((blocks, heads, 2 * DH, DH), lambda i: (i + start, 0, 0, 0)),
            pl.BlockSpec(memory_space=pl.ANY),
        ],
        out_specs=row,
        out_shape=jax.ShapeDtypeStruct((tokens, feats), F32),
        input_output_aliases={4: 0},
        cost_estimate=cost(8 * count * feats * BLK, 14 * count * feats),
        name="local_part",
    )(qkv, qkv, qkv, pre, att)


def norm_rows(q_ref, att_ref, pair, gain_ref, n_ref, h):
    cols = slice(h * DH, (h + 1) * DH)
    q = q_ref[:, cols]
    att = att_ref[:, cols] + dot(jnp.concatenate([q, q], axis=1), pair)
    mean_sq = jnp.mean(att * att, axis=-1, keepdims=True)
    n_ref[:, cols] = (att * lax.rsqrt(mean_sq + 1e-06) * gain_ref[:, cols]).astype(BF16)


def start_kernel(
    head, core, q_ref, att_ref, core_ref, mine_ref, partner_ref, gain_ref, n_ref, pair_ref
):
    heads = core_ref.shape[0]
    half = heads // 2
    for h in range(heads):

        @pl.when(pl.program_id(0) == 0)
        def _():
            carried = jnp.where(core[0] == 1, core_ref[h].astype(F32), 0.0)
            carried = carried + jnp.where(
                core[0] == h // half, mine_ref[h % half], partner_ref[h % half]
            )
            pair_ref[h] = hi_lo(carried)

    for h in range(heads):
        norm_rows(q_ref, att_ref, pair_ref[h], gain_ref, n_ref, h)


def finish_kernel(head, core, q_ref, att_ref, pair_ref, gain_ref, n_ref):
    for h in range(pair_ref.shape[0]):
        norm_rows(q_ref, att_ref, pair_ref[h], gain_ref, n_ref, h)


def finish(place, direction, shift, qkv, att, received, gain, parts, tile=256):
    _, tokens, feats = qkv.shape
    count = tokens // parts
    per = count // tile
    heads = feats // DH

    def row(i, head, core):
        to = head[0] + direction * (1 - 2 * core[0]) + shift + parts
        return (lax.rem(to, parts) * per + i, 0)

    first = len(received) > 1
    normed = jax.ShapeDtypeStruct((count, feats), BF16)
    rows = pl.BlockSpec((tile, feats), lambda i, *place: (i, 0))
    whole = lambda a: pl.BlockSpec(a.shape, lambda i, *place: (0,) * len(a.shape))
    pair = jax.ShapeDtypeStruct((heads, 2 * DH, DH), BF16)
    return pl.pallas_call(
        start_kernel if first else finish_kernel,
        grid_spec=pltpu.PrefetchScalarGridSpec(
            num_scalar_prefetch=2,
            grid=(per,),
            in_specs=[
                pl.BlockSpec((None, tile, feats), lambda *at: (0, *row(*at))),
                pl.BlockSpec((tile, feats), row),
            ]
            + [whole(a) for a in received]
            + [whole(gain)],
            out_specs=[rows, whole(pair)] if first else rows,
        ),
        out_shape=[normed, pair] if first else normed,
        cost_estimate=cost(2 * count * feats * DH * 2, count * feats * 8),
        name="finish",
    )(*place, qkv, att, *received, gain)


def own_kernel(n_ref, w_ref, *rest):
    later, (acc_ref, *passed, sem) = rest[: len(rest) // 2 - 1], rest[len(rest) // 2 - 1 :]
    copies = [
        pltpu.make_async_copy(source, target, sem.at[i])
        for i, (source, target) in enumerate(zip(later, passed))
    ]

    @pl.when(pl.program_id(0) == 0)
    def _():
        for copy in copies:
            copy.start()

    acc_ref[...] = dot(n_ref[...], w_ref[...])

    @pl.when(pl.program_id(0) == pl.num_programs(0) - 1)
    def _():
        for copy in copies:
            copy.wait()


def mix_own(normed, weight, later, tile=512):
    rows, feats = normed.shape
    width = weight.shape[1]
    anywhere = [pl.BlockSpec(memory_space=pl.ANY)] * len(later)
    return pl.pallas_call(
        own_kernel,
        grid=(width // tile,),
        in_specs=[
            pl.BlockSpec((rows, feats), lambda i: (0, 0)),
            pl.BlockSpec((feats, tile), lambda i: (0, i)),
        ]
        + anywhere,
        out_specs=[pl.BlockSpec((rows, tile), lambda i: (0, i))] + anywhere,
        out_shape=[jax.ShapeDtypeStruct((rows, width), F32)]
        + [jax.ShapeDtypeStruct(a.shape, a.dtype) for a in later],
        scratch_shapes=[pltpu.SemaphoreType.DMA((len(later),))],
        cost_estimate=cost(2 * rows * feats * width, 8 * rows * width),
        compiler_params=pltpu.CompilerParams(vmem_limit_bytes=24 << 20),
        name="mix_own",
    )(normed, weight, *later)


def middle_kernel(acc_ref, n_ref, w_ref, out_ref):
    out_ref[...] = acc_ref[...] + dot(n_ref[...], w_ref[...])


def mix_middle(acc, normed, weight, tile=1024):
    rows, feats = normed.shape
    width = acc.shape[1]
    column = lambda a: pl.BlockSpec((a.shape[0], tile), lambda i: (0, i))
    return pl.pallas_call(
        middle_kernel,
        grid=(width // tile,),
        in_specs=[column(acc), pl.BlockSpec((rows, feats), lambda i: (0, 0)), column(weight)],
        out_specs=column(acc),
        out_shape=jax.ShapeDtypeStruct((rows, width), F32),
        input_output_aliases={0: 0},
        cost_estimate=cost(2 * rows * feats * width, 8 * rows * width),
        compiler_params=pltpu.CompilerParams(vmem_limit_bytes=24 << 20),
        name="mix_middle",
    )(acc, normed, weight)


def last_kernel(core, acc_ref, nf, mine_ref, other_ref, out_ref):
    half = mine_ref.shape[0]
    mine = pl.multiple_of(core[0] * half, half)
    other = pl.multiple_of((1 - core[0]) * half, half)
    acc = dot(nf[:, pl.ds(mine, half)], mine_ref[...])
    acc += dot(nf[:, pl.ds(other, half)], other_ref[...])
    out_ref[...] = (acc + acc_ref[...]).astype(BF16)


def mix_last(core, acc, normed, weights, tile=2048):
    rows, feats = normed[0].shape
    width = acc.shape[1]
    column = lambda a: pl.BlockSpec((a.shape[0], tile), lambda i, core: (0, i))
    return pl.pallas_call(
        last_kernel,
        grid_spec=pltpu.PrefetchScalarGridSpec(
            num_scalar_prefetch=1,
            grid=(width // tile,),
            in_specs=[column(acc)]
            + [pl.BlockSpec(a.shape, lambda i, core: (0, 0)) for a in normed]
            + [column(a) for a in weights],
            out_specs=pl.BlockSpec((rows, tile), lambda i, core: (0, i)),
        ),
        out_shape=jax.ShapeDtypeStruct((rows, width), BF16),
        cost_estimate=cost(2 * rows * feats * width, 8 * rows * width),
        compiler_params=pltpu.CompilerParams(vmem_limit_bytes=24 << 20),
        name="mix_last",
    )(core, acc, *normed, *weights)


def pair_up(size, stride, total, first):
    pairs = []
    for i in range(total):
        at = (i // stride) % size
        to = at ^ 1 if first else (at + (1 if at % 2 else -1)) % size
        pairs.append((i, i + (to - at) * stride))
    return pairs


def pair_rounds(value, stride, total):
    value = value.astype(BF16)
    other = lax.ppermute(value, "seq", pair_up(4, stride, total, True))
    pair = (value.astype(F32) + other.astype(F32)).astype(BF16)
    far = lax.ppermute(pair, "seq", pair_up(4, stride, total, False))
    return other, far, pair.astype(F32) + far.astype(F32)


def layer(inputs, w_qkv, norm_gain, w_out):
    parts = lax.axis_size("head")
    total = lax.axis_size("seq")
    seq = lax.axis_index("seq")
    core = lax.rem(seq, 2)
    y = lax.rem(seq // 2, 4)
    x = seq // 8
    head = lax.axis_index("head")
    core_id = core.astype(jnp.int32).reshape(1)
    place = [a.astype(jnp.int32).reshape(1) for a in (head, core)]

    def along(direction):
        pairs = []
        for i in range(total):
            shift = direction * (1 - 2 * (i % 2))
            for h in range(parts):
                pairs.append((i * parts + h, i * parts + (h + shift) % parts))
        return pairs

    partner = [(i, i ^ 1) for i in range(total)]

    def swap(a):
        return lax.ppermute(a, "seq", partner)

    def send(a, direction):
        return lax.ppermute(a, ("seq", "head"), along(direction))

    near = send(w_out, 1)
    rows = w_out.shape[0] // 2
    far = lax.dynamic_slice_in_dim(near, core * rows, rows, 0)
    far = send(far, 1)
    near_other = swap(near)
    far_other = swap(far)

    qkv, pre, tot, att = project(inputs, w_qkv, 1)
    other = swap(tot)
    for piece in range(1, 4):
        att = local_part(qkv, pre, att, piece, 4)
    chip = tot.astype(F32) + other.astype(F32)
    half = chip.shape[0] // 2
    chip = lax.dynamic_slice_in_dim(chip, core * half, half, 0)
    y1, y2, row = pair_rounds(chip, 2, total)
    x1, x2, _ = pair_rounds(row, 8, total)
    takes = (
        (lax.rem(y, 2) == 1, y1),
        (y >= 2, y2),
        (lax.rem(x, 2) == 1, x1),
        (x >= 2, x2),
    )
    mine = sum(jnp.where(take, part.astype(F32), 0.0) for take, part in takes)
    received = (other, mine, swap(mine))

    gain = norm_gain.reshape(1, -1)
    nf, pair = finish(place, 0, 2, qkv, att, received, gain, parts)
    nf = send(nf, 1)
    na = send(finish(place, 1, 0, qkv, att, (pair,), gain, parts), 1)
    nb = send(finish(place, -1, 0, qkv, att, (pair,), gain, parts), -1)
    nf = send(nf, 1)
    n0 = finish(place, 0, 0, qkv, att, (pair,), gain, parts)
    acc, near, near_other, *weights = mix_own(n0, w_out, [near, near_other, far, far_other])
    acc = mix_middle(acc, na, near)
    acc = mix_middle(acc, nb, near_other)
    return mix_last(core_id, acc, [nf], weights)


def solution(mesh):
    return jax.shard_map(
        layer,
        mesh=mesh,
        in_specs=(P("seq", None), P(None, None, "head"), P("head"), P("head", None)),
        out_specs=P(("seq", "head"), None),
        check_vma=False,
    )
```
